32 devices in a mesh: groups: 2 (over x), seq: 16 (over z, y, core).
Axes of the slice: x: 2, y: 2, z: 4, core: 2. Of those that a mesh axis runs over, the one named last changes fastest.
Arguments:
- tokens: bfloat16 [4096, 1152], P(('groups', 'seq')), parts along dimension 0, may hold values from -30 to 30
- shift_cond: float32 [2304], P('groups'), parts along dimension 0, may hold values from -3 to 3
- scale_cond: float32 [2304], P('groups'), parts along dimension 0, may hold values from -3 to 3
- gate_cond: float32 [2304], P('groups'), parts along dimension 0, may hold values from -4 to 4
- qkv_weight: bfloat16 [1152, 3456], replicated, may hold values from -2 to 2
- out_weight: bfloat16 [1152, 1152], replicated, may hold values from -0.1875 to 0.1875
- cotangent: bfloat16 [4096, 1152], P(('groups', 'seq')), parts along dimension 0, may hold values from -6 to 6
Outputs:
- block_output: bfloat16 [4096, 1152], P(('groups', 'seq')), parts along dimension 0
- grad_input: bfloat16 [4096, 1152], P(('groups', 'seq')), parts along dimension 0
- grad_condition: float32 [6, 1152], P('groups'), parts along dimension 0
The draws below stay inside these ranges and needn't reach their ends.
There are 2 independent parts, one for each index of `groups`. The reference program is written for one: setup_inputs(seed, part) draws one part's arguments, and reference() takes and returns one part's arrays. A program takes and returns all parts, laid end to end along the dimension named above; an argument that names none is the same for every part. Nothing has to cross between parts.
All inputs are finite; a program needn't handle non-finite values.
Results may differ from the reference program's by a relative error of at most 0.012.
The reference program's roundings to bfloat16 on the way count: a program that leaves them out, or rounds other values in their place, can miss the bound.
Values may be sent and summed in bfloat16 or wider, within the bound.
No kernel may reach another device: no remote copies, remote signals or barrier semaphores. Data moves between devices by JAX's collectives and lax.ppermute only.
A program may use at most 128 MiB of HBM per device.

```python
import math
import jax
import jax.numpy as jnp
from jax import lax

D = 1152
H = 16
TOKENS = 2048


def draw_tokens(key, part):
    first_key, second_key = jax.random.split(key, 2)
    row_scale = jnp.exp(jax.random.uniform(second_key, (TOKENS, 1), jnp.float32, math.log(0.5), math.log(5.0)))
    base_values = jnp.clip(jax.random.normal(first_key, (TOKENS, D), jnp.float32), -4.0, 4.0)
    return (base_values * row_scale).astype(jnp.bfloat16)


def draw_qkv_weight(key, part):
    first_key = jax.random.fold_in(key, 0)
    base_values = jnp.clip(jax.random.normal(first_key, (D, 3 * D), jnp.float32), -4.0, 4.0)
    merged = jnp.concatenate([base_values[:, :2 * D] * 1.5, base_values[:, 2 * D:]], axis=1)
    return (merged / math.sqrt(D)).astype(jnp.bfloat16)


def block_levels(key, dims, cuts, smallest, largest):
    def one(dim, shards_of):
        steps = jax.random.uniform(jax.random.fold_in(jax.random.fold_in(key, 6), dim), (shards_of,), jnp.float32, smallest / len(cuts), largest / len(cuts))
        return jnp.repeat(jnp.exp(steps), dims[dim] // shards_of).reshape((-1,) + (1,) * (len(dims) - dim - 1))

    factor_of = one(*cuts[0])
    for cut in cuts[1:]:
        factor_of = factor_of * one(*cut)
    return factor_of


def noise(key, dims, scale, limit, pieces=(), held_as=jnp.bfloat16):
    result = jax.random.normal(key, dims, jnp.float32) * scale
    if len(pieces) > 0:
        result = block_levels(key, dims, pieces, -0.22, 0.18) * result
    return jnp.clip(result, min=-limit, max=limit).astype(held_as)


def setup_inputs(seed: int = 0, part: int = 0) -> dict:
    streams_of = jax.random.split(jax.random.key(seed), 8)
    part_splits = jax.random.split(jax.random.fold_in(streams_of[7], part), 8)
    return {
        "tokens": draw_tokens(jax.random.fold_in(jax.random.fold_in(streams_of[7], part), 71), part),
        "shift_cond": noise(part_splits[1], (D,), 0.5, 3.0, (), jnp.float32),
        "scale_cond": noise(part_splits[2], (D,), 0.5, 3.0, (), jnp.float32),
        "gate_cond": noise(part_splits[3], (D,), 1.0, 4.0, (), jnp.float32),
        "qkv_weight": draw_qkv_weight(jax.random.fold_in(streams_of[7], 71), part),
        "out_weight": noise(streams_of[5], (D, D), D ** -0.5, 0.1875),
        "cotangent": noise(part_splits[6], (TOKENS, D), 1.0, 6.0, ((0, 16),)),
    }


def head_weights(queries, key_rows, att_scale):
    scores = jnp.dot(queries, key_rows.T, preferred_element_type=jnp.float32) * att_scale
    row_max = lax.optimization_barrier(jnp.max(scores, axis=1, keepdims=True))
    exponent = jnp.exp(scores - row_max)
    return (exponent / lax.optimization_barrier(jnp.sum(exponent, axis=1, keepdims=True))).astype(jnp.bfloat16)

def reference(tokens, shift_cond, scale_cond, gate_cond, qkv_weight, out_weight, cotangent):
    head_size = D // H
    att_scale = 1.0 / math.sqrt(head_size)
    tokens_wide = tokens.astype(jnp.float32)
    row_mean = lax.optimization_barrier(jnp.mean(tokens_wide, axis=1, keepdims=True))
    centered = tokens_wide - row_mean
    variance = lax.optimization_barrier(jnp.mean(centered * centered, axis=1, keepdims=True))
    inv_std = lax.rsqrt(variance + 1e-06)
    normed = centered * inv_std
    modulated = (normed * (1.0 + scale_cond) + shift_cond).astype(jnp.bfloat16)
    qkv = jnp.dot(modulated, qkv_weight, preferred_element_type=jnp.float32).astype(jnp.bfloat16)
    head_parts = qkv.reshape(TOKENS, 3, H, head_size).transpose(2, 1, 0, 3)

    def forward_head(head_part):
        weights = head_weights(head_part[0], head_part[1], att_scale)
        return jnp.dot(weights, head_part[2], preferred_element_type=jnp.float32).astype(jnp.bfloat16)
    head_out = lax.map(forward_head, head_parts)
    attended = head_out.transpose(1, 0, 2).reshape(TOKENS, D)
    branch = jnp.dot(attended, out_weight, preferred_element_type=jnp.float32)
    block_output = (tokens_wide + gate_cond * branch).astype(jnp.bfloat16)
    cot_wide = cotangent.astype(jnp.float32)
    gated_grad = (gate_cond * cot_wide).astype(jnp.bfloat16)
    gate_grad = lax.optimization_barrier(jnp.sum(cot_wide * branch, axis=0))
    attended_grad = jnp.dot(gated_grad, out_weight.T, preferred_element_type=jnp.float32).astype(jnp.bfloat16)
    head_grads = attended_grad.reshape(TOKENS, H, head_size).transpose(1, 0, 2)

    def backward_head(block_items):
        head_part, out_grad, head_result = block_items
        queries, key_rows, value_rows = (head_part[0], head_part[1], head_part[2])
        weights = head_weights(queries, key_rows, att_scale)
        value_grad = jnp.dot(weights.T, out_grad, preferred_element_type=jnp.float32).astype(jnp.bfloat16)
        prob_grad = jnp.dot(out_grad, value_rows.T, preferred_element_type=jnp.float32)
        row_delta = lax.optimization_barrier(jnp.sum(head_result.astype(jnp.float32) * out_grad.astype(jnp.float32), axis=1, keepdims=True))
        score_grad = (weights.astype(jnp.float32) * (prob_grad - row_delta) * att_scale).astype(jnp.bfloat16)
        query_grad = jnp.dot(score_grad, key_rows, preferred_element_type=jnp.float32).astype(jnp.bfloat16)
        key_grad = jnp.dot(score_grad.T, queries, preferred_element_type=jnp.float32).astype(jnp.bfloat16)
        return jnp.stack([query_grad, key_grad, value_grad])
    all_grads = lax.map(backward_head, (head_parts, head_grads, head_out))
    qkv_grad = all_grads.transpose(2, 1, 0, 3).reshape(TOKENS, 3 * D)
    modulated_grad = jnp.dot(qkv_grad, qkv_weight.T, preferred_element_type=jnp.float32)
    shift_grad = lax.optimization_barrier(jnp.sum(modulated_grad, axis=0))
    scale_grad = lax.optimization_barrier(jnp.sum(modulated_grad * normed, axis=0))
    grad_condition = jnp.stack([shift_grad, scale_grad, gate_grad]) / math.sqrt(TOKENS)
    normed_grad = modulated_grad * (1.0 + scale_cond)
    first_mean = lax.optimization_barrier(jnp.mean(normed_grad, axis=1, keepdims=True))
    second_mean = lax.optimization_barrier(jnp.mean(normed_grad * normed, axis=1, keepdims=True))
    grad_input = (cot_wide + inv_std * (normed_grad - first_mean - normed * second_mean)).astype(jnp.bfloat16)
    return (block_output, grad_input, grad_condition)
```

```python
import functools
import math

import jax
import jax.numpy as jnp
from jax import lax
from jax.experimental import pallas as pl
from jax.experimental.pallas import tpu as pltpu
from jax.sharding import PartitionSpec as P

H = 16
LANES = 128
F32 = jnp.float32
BF16 = jnp.bfloat16
VMEM_LIMIT = 56 * 1024 * 1024


def params():
    return pltpu.CompilerParams(
        dimension_semantics=("arbitrary",), vmem_limit_bytes=VMEM_LIMIT
    )


def normalise(tokens):
    wide = tokens.astype(F32)
    row_mean = jnp.mean(wide, axis=1, keepdims=True)
    centered = wide - row_mean
    variance = jnp.mean(centered * centered, axis=1, keepdims=True)
    inv_std = lax.rsqrt(variance + 1e-06)
    return wide, centered * inv_std, inv_std


def project_kernel(
    head_size, tokens, shift, scale, gate, qkv_w, out_w, cot, packed, modulated, gated, flat
):
    step = pl.program_id(0)
    width = tokens.shape[1]
    tile = qkv_w.shape[1]
    rows = out_w.shape[0]

    @pl.when(step == 0)
    def _():
        _, normed, _ = normalise(tokens[...])
        modulated[...] = (normed * (1.0 + scale[...]) + shift[...]).astype(BF16)
        gated[...] = (gate[...] * cot[...].astype(F32)).astype(BF16)

    cols = jnp.dot(modulated[...], qkv_w[...], preferred_element_type=F32)
    flat[pl.ds(pl.multiple_of(step * tile, LANES), tile), :] = cols.T
    flat[pl.ds(pl.multiple_of(3 * width + step * rows, LANES), rows), :] = lax.dot_general(
        out_w[...], gated[...], (((1,), (1,)), ((), ())), preferred_element_type=F32
    )

    @pl.when(step == pl.num_programs(0) - 1)
    def _():
        for head in range(H):
            packed[head] = jnp.concatenate(
                [
                    flat[part * width + head * head_size : part * width + (head + 1) * head_size, :]
                    for part in range(4)
                ],
                axis=0,
            ).astype(BF16)


def project(tokens, shift, scale, gate, qkv_w, out_w, cot):
    tok_rows, width = tokens.shape
    steps = width // LANES
    head_size = width // H
    tile = 3 * LANES
    whole = lambda shape: pl.BlockSpec(shape, lambda i: (0,) * len(shape))
    return pl.pallas_call(
        functools.partial(project_kernel, head_size),
        grid=(steps,),
        in_specs=[
            whole((tok_rows, width)),
            whole((1, width)),
            whole((1, width)),
            whole((1, width)),
            pl.BlockSpec((width, tile), lambda i: (0, i)),
            pl.BlockSpec((LANES, width), lambda i: (i, 0)),
            whole((tok_rows, width)),
        ],
        out_specs=whole((H, 4 * head_size, tok_rows)),
        out_shape=jax.ShapeDtypeStruct((H, 4 * head_size, tok_rows), BF16),
        scratch_shapes=[
            pltpu.VMEM((tok_rows, width), BF16),
            pltpu.VMEM((tok_rows, width), BF16),
            pltpu.VMEM((4 * width, tok_rows), F32),
        ],
        compiler_params=params(),
        name="project",
    )(tokens, shift, scale, gate, qkv_w, out_w, cot)


def attend_kernel(head_size, group, split, items, *refs):
    if split:
        pairs, near, far = refs[:3]
        refs = refs[3:]
    else:
        near = refs[0]
        refs = refs[1:]
    key_rows, value_rows, key_cols, value_cols, key_grad, value_grad, near_flat = refs
    step = pl.program_id(0)
    chunks = items.shape[0]
    key_chunks = key_rows.shape[0] // LANES
    att_scale = 1.0 / math.sqrt(head_size)
    pad = value_rows.shape[1] - head_size

    @pl.when(step == 0)
    def _():
        for s in range(key_chunks):
            if split:
                pair = pairs[s].astype(F32)
            else:
                pair = items[s].astype(F32)[head_size : 3 * head_size]
            at = slice(s * LANES, (s + 1) * LANES)
            keys, values = pair[:head_size], pair[head_size:]
            key_cols[:, at] = keys.astype(BF16)
            value_cols[:, at] = values.astype(BF16)
            key_rows[at, :] = keys.T.astype(BF16)
            value_rows[at, :] = jnp.concatenate(
                [values, jnp.ones((pad, LANES), F32)], axis=0
            ).T.astype(BF16)
        key_grad[...] = jnp.zeros_like(key_grad)
        value_grad[...] = jnp.zeros_like(value_grad)

    block = [items[step * group + g].astype(F32) for g in range(group)]
    queries = jnp.concatenate([b[:head_size] for b in block], axis=1)
    grads = jnp.concatenate([b[3 * head_size :] for b in block], axis=1)
    scores = jnp.dot(key_rows[...], queries.astype(BF16), preferred_element_type=F32) * att_scale
    row_max = jnp.max(scores, axis=0, keepdims=True)
    exponent = jnp.exp(scores - row_max)
    total = jnp.sum(exponent, axis=0, keepdims=True)
    weights = (exponent * (1.0 / total)).astype(BF16)
    attended = (
        jnp.dot(value_cols[...], weights, preferred_element_type=F32).astype(BF16).astype(F32)
    )
    less = -jnp.sum(attended * grads, axis=0, keepdims=True)
    less_high = less.astype(BF16).astype(F32)
    less_mid = (less - less_high).astype(BF16).astype(F32)
    less_low = less - less_high - less_mid
    place = lax.broadcasted_iota(jnp.int32, (pad, less.shape[1]), 0)
    tail = jnp.where(
        place == 0, less_high, jnp.where(place == 1, less_mid, jnp.where(place == 2, less_low, 0.0))
    )
    centred_grad = jnp.dot(
        value_rows[...],
        jnp.concatenate([grads, tail], axis=0).astype(BF16),
        preferred_element_type=F32,
    )
    score_grad = (weights.astype(F32) * centred_grad * att_scale).astype(BF16)
    query_grad = jnp.dot(key_cols[...], score_grad, preferred_element_type=F32)
    key_grad[...] += jnp.dot(score_grad, queries.T.astype(BF16), preferred_element_type=F32)
    value_grad[...] += jnp.dot(weights, grads.T.astype(BF16), preferred_element_type=F32)
    for g in range(group):
        at = slice(g * LANES, (g + 1) * LANES)
        near_flat[step * group + g] = jnp.concatenate(
            [attended[:, at], query_grad[:, at]], axis=0
        )

    @pl.when(step == pl.num_programs(0) - 1)
    def _():
        for s in range(key_chunks):
            at = slice(s * LANES, (s + 1) * LANES)
            grads_of = jnp.concatenate([key_grad[at, :].T, value_grad[at, :].T], axis=0)
            if split:
                far[s] = grads_of
            else:
                near[s] = jnp.concatenate([near_flat[s], grads_of], axis=0).astype(BF16)
        if split:
            near[...] = near_flat[...].astype(BF16)


def attend(items, pairs=None):
    chunks = items.shape[0]
    head_size = items.shape[1] // 4
    split = pairs is not None
    key_chunks = pairs.shape[0] if split else chunks
    group = 2 if chunks % 2 == 0 else 1
    key_len = key_chunks * LANES
    pad = 8
    whole = lambda shape: pl.BlockSpec(shape, lambda i: (0,) * len(shape))
    if split:
        shapes = [
            jax.ShapeDtypeStruct((chunks, 2 * head_size, LANES), BF16),
            jax.ShapeDtypeStruct((key_chunks, 2 * head_size, LANES), F32),
        ]
        operands = (items, pairs)
    else:
        shapes = [jax.ShapeDtypeStruct((chunks, 4 * head_size, LANES), BF16)]
        operands = (items,)
    return pl.pallas_call(
        functools.partial(attend_kernel, head_size, group, split),
        grid=(chunks // group,),
        in_specs=[whole(x.shape) for x in operands],
        out_specs=[whole(x.shape) for x in shapes],
        out_shape=shapes,
        scratch_shapes=[
            pltpu.VMEM((key_len, head_size), BF16),
            pltpu.VMEM((key_len, head_size + pad), BF16),
            pltpu.VMEM((head_size, key_len), BF16),
            pltpu.VMEM((head_size, key_len), BF16),
            pltpu.VMEM((key_len, head_size), F32),
            pltpu.VMEM((key_len, head_size), F32),
            pltpu.VMEM((chunks, 2 * head_size, LANES), F32),
        ],
        compiler_params=params(),
        name="attend",
    )(*operands)


def finish_kernel(
    head_size, items, tokens, scale, gate, qkv_w, out_w, cot,
    block_output, grad_input, sums, att_cols, grad_cols, branch, mod_grad,
):
    step = pl.program_id(0)
    width = tokens.shape[1]
    rows = qkv_w.shape[0]

    @pl.when(step == 0)
    def _():
        flat = [items[head].astype(F32) for head in range(H)]
        att = jnp.concatenate([x[:head_size] for x in flat], axis=0)
        for part in range(width // LANES):
            att_cols[part] = att[part * LANES : (part + 1) * LANES, :].T.astype(BF16)
        for part in range(3):
            grad_cols[part * width : (part + 1) * width, :] = jnp.concatenate(
                [x[(part + 1) * head_size : (part + 2) * head_size] for x in flat], axis=0
            ).astype(BF16)
        branch[...] = jnp.zeros_like(branch)

    branch[...] += jnp.dot(att_cols[step], out_w[...], preferred_element_type=F32)
    mod_grad[step] = jnp.dot(qkv_w[...], grad_cols[...], preferred_element_type=F32).T

    @pl.when(step == pl.num_programs(0) - 1)
    def _():
        wide, normed, inv_std = normalise(tokens[...])
        cot_wide = cot[...].astype(F32)
        out = branch[...]
        block_output[...] = (wide + gate[...] * out).astype(BF16)
        back = jnp.concatenate([mod_grad[i] for i in range(width // rows)], axis=1)
        sums[...] = jnp.concatenate(
            [
                jnp.sum(back, axis=0, keepdims=True),
                jnp.sum(back * normed, axis=0, keepdims=True),
                jnp.sum(cot_wide * out, axis=0, keepdims=True),
            ],
            axis=0,
        )
        normed_grad = back * (1.0 + scale[...])
        first_mean = jnp.mean(normed_grad, axis=1, keepdims=True)
        second_mean = jnp.mean(normed_grad * normed, axis=1, keepdims=True)
        grad_input[...] = (
            cot_wide + inv_std * (normed_grad - first_mean - normed * second_mean)
        ).astype(BF16)


def finish(items, tokens, scale, gate, qkv_w, out_w, cot):
    tok_rows, width = tokens.shape
    head_size = width // H
    steps = width // LANES
    whole = lambda shape: pl.BlockSpec(shape, lambda i: (0,) * len(shape))
    return pl.pallas_call(
        functools.partial(finish_kernel, head_size),
        grid=(steps,),
        in_specs=[
            whole(items.shape),
            whole((tok_rows, width)),
            whole((1, width)),
            whole((1, width)),
            pl.BlockSpec((LANES, 3 * width), lambda i: (i, 0)),
            pl.BlockSpec((LANES, width), lambda i: (i, 0)),
            whole((tok_rows, width)),
        ],
        out_specs=[whole((tok_rows, width)), whole((tok_rows, width)), whole((3, width))],
        out_shape=[
            jax.ShapeDtypeStruct((tok_rows, width), BF16),
            jax.ShapeDtypeStruct((tok_rows, width), BF16),
            jax.ShapeDtypeStruct((3, width), F32),
        ],
        scratch_shapes=[
            pltpu.VMEM((steps, tok_rows, LANES), BF16),
            pltpu.VMEM((3 * width, tok_rows), BF16),
            pltpu.VMEM((tok_rows, width), F32),
            pltpu.VMEM((steps, tok_rows, LANES), F32),
        ],
        compiler_params=params(),
        name="finish",
    )(items, tokens, scale, gate, qkv_w, out_w, cot)


def from_partner(shard, axis, stride):
    return lax.ppermute(shard, axis, [(i, i ^ stride) for i in range(lax.axis_size(axis))])


def exchange(blocks):
    return lax.all_to_all(blocks, "seq", split_axis=0, concat_axis=0, tiled=True)


def per_device(tokens, shift_cond, scale_cond, gate_cond, qkv_weight, out_weight, cotangent):
    seq_count = lax.axis_size("seq")
    repeat = seq_count // H
    levels = repeat.bit_length() - 1
    tok_rows, width = tokens.shape
    head_size = width // H
    sub_rows = tok_rows // repeat
    shift, scale, gate = (x.reshape(1, width) for x in (shift_cond, scale_cond, gate_cond))
    packed = project(tokens, shift, scale, gate, qkv_weight, out_weight, cotangent)
    if repeat == 1:
        (made,) = attend(exchange(packed))
        returned = exchange(made)
    else:
        packed = packed.reshape(H, 4 * head_size, repeat, sub_rows).transpose(0, 2, 1, 3)
        landed = exchange(packed.reshape(seq_count, 4 * head_size, sub_rows))
        items = landed.reshape(H, repeat, 4 * head_size, sub_rows).transpose(0, 2, 1, 3)
        items = items.reshape(H, 4 * head_size, tok_rows)
        pairs = items[:, head_size : 3 * head_size]
        for level in range(levels):
            pairs = jnp.concatenate([pairs, from_partner(pairs, "seq", 1 << level)], axis=0)
        near, far = attend(items, pairs)
        for level in reversed(range(levels)):
            middle = far.shape[0] // 2
            far = far[:middle] + from_partner(far[middle:], "seq", 1 << level)
        made = jnp.concatenate([near, far.astype(BF16)], axis=1)
        made = made.reshape(H, 4 * head_size, repeat, sub_rows).transpose(0, 2, 1, 3)
        back = exchange(made.reshape(seq_count, 4 * head_size, sub_rows))
        returned = back.reshape(H, repeat, 4 * head_size, sub_rows).transpose(0, 2, 1, 3)
        returned = returned.reshape(H, 4 * head_size, tok_rows)
    block_output, grad_input, sums = finish(
        returned, tokens, scale, gate, qkv_weight, out_weight, cotangent
    )
    stride = 1
    while stride < seq_count:
        sums = sums + from_partner(sums, "seq", stride)
        stride *= 2
    grad_condition = sums / math.sqrt(tok_rows * seq_count)
    return (block_output, grad_input, grad_condition)


def solution(mesh):
    return jax.shard_map(
        per_device,
        mesh=mesh,
        in_specs=(
            P(("groups", "seq"), None),
            P("groups"),
            P("groups"),
            P("groups"),
            P(),
            P(),
            P(("groups", "seq"), None),
        ),
        out_specs=(P(("groups", "seq"), None), P(("groups", "seq"), None), P("groups", None)),
        check_vma=False,
    )
```

```python
import functools
import math

import jax
import jax.numpy as jnp
from jax import lax
from jax.experimental import pallas as pl
from jax.experimental.pallas import tpu as pltpu
from jax.sharding import PartitionSpec as P

H = 16
LANES = 128
STEPS = 3
SCORE_LIMIT = 2048 * 2048
F32 = jnp.float32
BF16 = jnp.bfloat16
VMEM_LIMIT = 60 * 1024 * 1024


def params():
    return pltpu.CompilerParams(
        dimension_semantics=("arbitrary",), vmem_limit_bytes=VMEM_LIMIT
    )


def row(vector):
    return vector[...].reshape(1, vector.shape[0])


def normalise(tokens):
    wide = tokens.astype(F32)
    row_mean = jnp.mean(wide, axis=1, keepdims=True)
    centered = wide - row_mean
    variance = jnp.mean(centered * centered, axis=1, keepdims=True)
    inv_std = lax.rsqrt(variance + 1e-06)
    return wide, centered * inv_std, inv_std


def project_kernel(
    head_size, tokens, shift, scale, gate, qkv_w, out_w, cot, packed, modulated, gated, flat
):
    step = pl.program_id(0)
    width = tokens.shape[1]
    tile = qkv_w.shape[1]
    rows = out_w.shape[0]

    @pl.when(step == 0)
    def _():
        _, normed, _ = normalise(tokens[...])
        modulated[...] = (normed * (1.0 + row(scale)) + row(shift)).astype(BF16)
        gated[...] = (row(gate) * cot[...].astype(F32)).astype(BF16)

    cols = jnp.dot(modulated[...], qkv_w[...], preferred_element_type=F32)
    flat[pl.ds(pl.multiple_of(step * tile, LANES), tile), :] = cols.T
    flat[pl.ds(pl.multiple_of(3 * width + step * rows, LANES), rows), :] = lax.dot_general(
        out_w[...], gated[...], (((1,), (1,)), ((), ())), preferred_element_type=F32
    )

    @pl.when(step == pl.num_programs(0) - 1)
    def _():
        for head in range(H):
            packed[head] = jnp.concatenate(
                [
                    flat[part * width + head * head_size : part * width + (head + 1) * head_size, :]
                    for part in range(4)
                ],
                axis=0,
            ).astype(BF16)


def project(tokens, shift, scale, gate, qkv_w, out_w, cot):
    tok_rows, width = tokens.shape
    steps = STEPS
    head_size = width // H
    tile = 3 * width // steps
    whole = lambda shape: pl.BlockSpec(shape, lambda i: (0,) * len(shape))
    return pl.pallas_call(
        functools.partial(project_kernel, head_size),
        grid=(steps,),
        in_specs=[
            whole((tok_rows, width)),
            whole((width,)),
            whole((width,)),
            whole((width,)),
            pl.BlockSpec((width, tile), lambda i: (0, i)),
            pl.BlockSpec((width // steps, width), lambda i: (i, 0)),
            whole((tok_rows, width)),
        ],
        out_specs=whole((H, 4 * head_size, tok_rows)),
        out_shape=jax.ShapeDtypeStruct((H, 4 * head_size, tok_rows), BF16),
        scratch_shapes=[
            pltpu.VMEM((tok_rows, width), BF16),
            pltpu.VMEM((tok_rows, width), BF16),
            pltpu.VMEM((4 * width, tok_rows), F32),
        ],
        compiler_params=params(),
        name="project",
    )(tokens, shift, scale, gate, qkv_w, out_w, cot)


def attend_kernel(head_size, group, split, items, *refs):
    if split:
        pairs, near, far = refs[:3]
        refs = refs[3:]
    else:
        near = refs[0]
        refs = refs[1:]
    key_rows, value_rows, key_cols, value_cols, key_grad, value_grad, near_flat = refs
    step = pl.program_id(0)
    chunks = items.shape[0]
    key_chunks = key_rows.shape[0] // LANES
    att_scale = 1.0 / math.sqrt(head_size)
    exponent_scale = att_scale * math.log2(math.e)
    pad = value_rows.shape[1] - head_size

    @pl.when(step == 0)
    def _():
        for s in range(key_chunks):
            if split:
                pair = pairs[s].astype(F32)
            else:
                pair = items[s].astype(F32)[head_size : 3 * head_size]
            at = slice(s * LANES, (s + 1) * LANES)
            keys, values = pair[:head_size], pair[head_size:]
            key_cols[:, at] = keys.astype(BF16)
            value_cols[:, at] = values.astype(BF16)
            key_rows[at, :] = keys.T.astype(BF16)
            value_rows[at, :] = jnp.concatenate(
                [values, jnp.ones((pad, LANES), F32)], axis=0
            ).T.astype(BF16)
        key_grad[...] = jnp.zeros_like(key_grad)
        value_grad[...] = jnp.zeros_like(value_grad)

    block = [items[step * group + g].astype(F32) for g in range(group)]
    queries = jnp.concatenate([b[:head_size] for b in block], axis=1)
    grads = jnp.concatenate([b[3 * head_size :] for b in block], axis=1)
    scores = jnp.dot(key_rows[...], queries.astype(BF16), preferred_element_type=F32)
    row_max = jnp.max(scores, axis=0, keepdims=True)
    exponent = jnp.exp2((scores - row_max) * exponent_scale)
    total = jnp.sum(exponent, axis=0, keepdims=True)
    weights = (exponent * (1.0 / total)).astype(BF16)
    attended = (
        jnp.dot(value_cols[...], weights, preferred_element_type=F32).astype(BF16).astype(F32)
    )
    less = -jnp.sum(attended * grads, axis=0, keepdims=True)
    less_high = less.astype(BF16).astype(F32)
    less_mid = (less - less_high).astype(BF16).astype(F32)
    less_low = less - less_high - less_mid
    place = lax.broadcasted_iota(jnp.int32, (pad, less.shape[1]), 0)
    tail = jnp.where(
        place == 0, less_high, jnp.where(place == 1, less_mid, jnp.where(place == 2, less_low, 0.0))
    )
    centred_grad = jnp.dot(
        value_rows[...],
        jnp.concatenate([grads, tail], axis=0).astype(BF16),
        preferred_element_type=F32,
    )
    score_grad = (weights.astype(F32) * centred_grad * att_scale).astype(BF16)
    query_grad = jnp.dot(key_cols[...], score_grad, preferred_element_type=F32)
    key_grad[...] += jnp.dot(score_grad, queries.T.astype(BF16), preferred_element_type=F32)
    value_grad[...] += jnp.dot(weights, grads.T.astype(BF16), preferred_element_type=F32)
    for g in range(group):
        at = slice(g * LANES, (g + 1) * LANES)
        near_flat[step * group + g] = jnp.concatenate(
            [attended[:, at], query_grad[:, at]], axis=0
        )

    @pl.when(step == pl.num_programs(0) - 1)
    def _():
        for s in range(key_chunks):
            at = slice(s * LANES, (s + 1) * LANES)
            grads_of = jnp.concatenate([key_grad[at, :].T, value_grad[at, :].T], axis=0)
            if split:
                far[s] = grads_of
            else:
                near[s] = jnp.concatenate([near_flat[s], grads_of], axis=0).astype(BF16)
        if split:
            near[...] = near_flat[...].astype(BF16)


def attend(items, pairs=None):
    chunks = items.shape[0]
    head_size = items.shape[1] // 4
    split = pairs is not None
    key_chunks = pairs.shape[0] if split else chunks
    key_len = key_chunks * LANES
    group = math.gcd(chunks, max(1, SCORE_LIMIT // (key_len * LANES)))
    pad = 8
    whole = lambda shape: pl.BlockSpec(shape, lambda i: (0,) * len(shape))
    if split:
        shapes = [
            jax.ShapeDtypeStruct((chunks, 2 * head_size, LANES), BF16),
            jax.ShapeDtypeStruct((key_chunks, 2 * head_size, LANES), F32),
        ]
        operands = (items, pairs)
    else:
        shapes = [jax.ShapeDtypeStruct((chunks, 4 * head_size, LANES), BF16)]
        operands = (items,)
    return pl.pallas_call(
        functools.partial(attend_kernel, head_size, group, split),
        grid=(chunks // group,),
        in_specs=[whole(x.shape) for x in operands],
        out_specs=[whole(x.shape) for x in shapes],
        out_shape=shapes,
        scratch_shapes=[
            pltpu.VMEM((key_len, head_size), BF16),
            pltpu.VMEM((key_len, head_size + pad), BF16),
            pltpu.VMEM((head_size, key_len), BF16),
            pltpu.VMEM((head_size, key_len), BF16),
            pltpu.VMEM((key_len, head_size), F32),
            pltpu.VMEM((key_len, head_size), F32),
            pltpu.VMEM((chunks, 2 * head_size, LANES), F32),
        ],
        compiler_params=params(),
        name="attend",
    )(*operands)


def finish_kernel(
    head_size, items, tokens, scale, gate, qkv_w, out_w, cot,
    block_output, grad_input, sums, att_cols, grad_cols, branch, mod_grad,
):
    step = pl.program_id(0)
    width = tokens.shape[1]
    rows = qkv_w.shape[0]

    @pl.when(step == 0)
    def _():
        flat = [items[head].astype(F32) for head in range(H)]
        att = jnp.concatenate([x[:head_size] for x in flat], axis=0)
        for part in range(width // rows):
            att_cols[part] = att[part * rows : (part + 1) * rows, :].T.astype(BF16)
        for part in range(3):
            grad_cols[part * width : (part + 1) * width, :] = jnp.concatenate(
                [x[(part + 1) * head_size : (part + 2) * head_size] for x in flat], axis=0
            ).astype(BF16)
        branch[...] = jnp.zeros_like(branch)

    branch[...] += jnp.dot(att_cols[step], out_w[...], preferred_element_type=F32)
    mod_grad[step] = jnp.dot(qkv_w[...], grad_cols[...], preferred_element_type=F32).T

    @pl.when(step == pl.num_programs(0) - 1)
    def _():
        wide, normed, inv_std = normalise(tokens[...])
        cot_wide = cot[...].astype(F32)
        out = branch[...]
        block_output[...] = (wide + row(gate) * out).astype(BF16)
        back = jnp.concatenate([mod_grad[i] for i in range(width // rows)], axis=1)
        sums[...] = jnp.concatenate(
            [
                jnp.sum(back, axis=0, keepdims=True),
                jnp.sum(back * normed, axis=0, keepdims=True),
                jnp.sum(cot_wide * out, axis=0, keepdims=True),
            ],
            axis=0,
        )
        normed_grad = back * (1.0 + row(scale))
        first_mean = jnp.mean(normed_grad, axis=1, keepdims=True)
        second_mean = jnp.mean(normed_grad * normed, axis=1, keepdims=True)
        grad_input[...] = (
            cot_wide + inv_std * (normed_grad - first_mean - normed * second_mean)
        ).astype(BF16)


def finish(items, tokens, scale, gate, qkv_w, out_w, cot):
    tok_rows, width = tokens.shape
    head_size = width // H
    steps = STEPS
    whole = lambda shape: pl.BlockSpec(shape, lambda i: (0,) * len(shape))
    return pl.pallas_call(
        functools.partial(finish_kernel, head_size),
        grid=(steps,),
        in_specs=[
            whole(items.shape),
            whole((tok_rows, width)),
            whole((width,)),
            whole((width,)),
            pl.BlockSpec((width // steps, 3 * width), lambda i: (i, 0)),
            pl.BlockSpec((width // steps, width), lambda i: (i, 0)),
            whole((tok_rows, width)),
        ],
        out_specs=[whole((tok_rows, width)), whole((tok_rows, width)), whole((3, width))],
        out_shape=[
            jax.ShapeDtypeStruct((tok_rows, width), BF16),
            jax.ShapeDtypeStruct((tok_rows, width), BF16),
            jax.ShapeDtypeStruct((3, width), F32),
        ],
        scratch_shapes=[
            pltpu.VMEM((steps, tok_rows, width // steps), BF16),
            pltpu.VMEM((3 * width, tok_rows), BF16),
            pltpu.VMEM((tok_rows, width), F32),
            pltpu.VMEM((steps, tok_rows, width // steps), F32),
        ],
        compiler_params=params(),
        name="finish",
    )(items, tokens, scale, gate, qkv_w, out_w, cot)


def from_partner(shard, axis, stride):
    return lax.ppermute(shard, axis, [(i, i ^ stride) for i in range(lax.axis_size(axis))])


def exchange(blocks):
    return lax.all_to_all(blocks, "seq", split_axis=0, concat_axis=0, tiled=True)


def per_device(tokens, shift_cond, scale_cond, gate_cond, qkv_weight, out_weight, cotangent):
    seq_count = lax.axis_size("seq")
    repeat = seq_count // H
    levels = repeat.bit_length() - 1
    tok_rows, width = tokens.shape
    head_size = width // H
    sub_rows = tok_rows // repeat
    packed = project(tokens, shift_cond, scale_cond, gate_cond, qkv_weight, out_weight, cotangent)
    if repeat == 1:
        (made,) = attend(exchange(packed))
        returned = exchange(made)
    else:
        packed = packed.reshape(H, 4 * head_size, repeat, sub_rows).transpose(0, 2, 1, 3)
        landed = exchange(packed.reshape(seq_count, 4 * head_size, sub_rows))
        items = landed.reshape(H, repeat, 4 * head_size, sub_rows).transpose(0, 2, 1, 3)
        items = items.reshape(H, 4 * head_size, tok_rows)
        pairs = items[:, head_size : 3 * head_size]
        for level in range(levels):
            pairs = jnp.concatenate([pairs, from_partner(pairs, "seq", 1 << level)], axis=0)
        near, far = attend(items, pairs)
        for level in reversed(range(levels)):
            middle = far.shape[0] // 2
            far = far[:middle] + from_partner(far[middle:], "seq", 1 << level)
        made = jnp.concatenate([near, far.astype(BF16)], axis=1)
        made = made.reshape(H, 4 * head_size, repeat, sub_rows).transpose(0, 2, 1, 3)
        back = exchange(made.reshape(seq_count, 4 * head_size, sub_rows))
        returned = back.reshape(H, repeat, 4 * head_size, sub_rows).transpose(0, 2, 1, 3)
        returned = returned.reshape(H, 4 * head_size, tok_rows)
    block_output, grad_input, sums = finish(
        returned, tokens, scale_cond, gate_cond, qkv_weight, out_weight, cotangent
    )
    stride = 1
    while stride < seq_count:
        sums = sums + from_partner(sums, "seq", stride)
        stride *= 2
    grad_condition = sums / math.sqrt(tok_rows * seq_count)
    return (block_output, grad_input, grad_condition)


def solution(mesh):
    return jax.shard_map(
        per_device,
        mesh=mesh,
        in_specs=(
            P(("groups", "seq"), None),
            P("groups"),
            P("groups"),
            P("groups"),
            P(),
            P(),
            P(("groups", "seq"), None),
        ),
        out_specs=(P(("groups", "seq"), None), P(("groups", "seq"), None), P("groups", None)),
        check_vma=False,
    )
```

```python
import functools
import math

import jax
import jax.numpy as jnp
from jax import lax
from jax.experimental import pallas as pl
from jax.experimental.pallas import tpu as pltpu
from jax.sharding import PartitionSpec as P

H = 16
LANES = 128
STEPS = 3
SCORE_LIMIT = 2048 * 2048
F32 = jnp.float32
BF16 = jnp.bfloat16
PROJECT_LIMIT = 60 * 1024 * 1024
ATTEND_LIMIT = 44 * 1024 * 1024
FINISH_LIMIT = 24 * 1024 * 1024


def params(limit):
    return pltpu.CompilerParams(dimension_semantics=("arbitrary",), vmem_limit_bytes=limit)


def row(vector):
    return vector[...].reshape(1, vector.shape[0])


def normalise(tokens):
    wide = tokens.astype(F32)
    row_mean = jnp.mean(wide, axis=1, keepdims=True)
    centered = wide - row_mean
    variance = jnp.mean(centered * centered, axis=1, keepdims=True)
    inv_std = lax.rsqrt(variance + 1e-06)
    return wide, centered * inv_std, inv_std


def project_kernel(
    head_size, tokens, shift, scale, gate, qkv_w, out_w, cot, packed, modulated, gated, flat
):
    step = pl.program_id(0)
    width = tokens.shape[1]
    tile = qkv_w.shape[1]
    rows = out_w.shape[0]

    @pl.when(step == 0)
    def _():
        _, normed, _ = normalise(tokens[...])
        modulated[...] = (normed * (1.0 + row(scale)) + row(shift)).astype(BF16)
        gated[...] = (row(gate) * cot[...].astype(F32)).astype(BF16)

    cols = jnp.dot(modulated[...], qkv_w[...], preferred_element_type=F32)
    flat[pl.ds(pl.multiple_of(step * tile, LANES), tile), :] = cols.T
    flat[pl.ds(pl.multiple_of(3 * width + step * rows, LANES), rows), :] = lax.dot_general(
        out_w[...], gated[...], (((1,), (1,)), ((), ())), preferred_element_type=F32
    )

    @pl.when(step == pl.num_programs(0) - 1)
    def _():
        for head in range(H):
            packed[head] = jnp.concatenate(
                [
                    flat[part * width + head * head_size : part * width + (head + 1) * head_size, :]
                    for part in range(4)
                ],
                axis=0,
            ).astype(BF16)


def project(tokens, shift, scale, gate, qkv_w, out_w, cot):
    tok_rows, width = tokens.shape
    steps = STEPS
    head_size = width // H
    tile = 3 * width // steps
    whole = lambda shape: pl.BlockSpec(shape, lambda i: (0,) * len(shape))
    return pl.pallas_call(
        functools.partial(project_kernel, head_size),
        grid=(steps,),
        in_specs=[
            whole((tok_rows, width)),
            whole((width,)),
            whole((width,)),
            whole((width,)),
            pl.BlockSpec((width, tile), lambda i: (0, i)),
            pl.BlockSpec((width // steps, width), lambda i: (i, 0)),
            whole((tok_rows, width)),
        ],
        out_specs=whole((H, 4 * head_size, tok_rows)),
        out_shape=jax.ShapeDtypeStruct((H, 4 * head_size, tok_rows), BF16),
        scratch_shapes=[
            pltpu.VMEM((tok_rows, width), BF16),
            pltpu.VMEM((tok_rows, width), BF16),
            pltpu.VMEM((4 * width, tok_rows), F32),
        ],
        compiler_params=params(PROJECT_LIMIT),
        name="project",
    )(tokens, shift, scale, gate, qkv_w, out_w, cot)


def attend_kernel(head_size, group, split, items, weight, *refs):
    if split:
        pairs, held, near, far = refs[:4]
        refs = refs[4:]
    else:
        held, near = refs[:2]
        refs = refs[2:]
    key_rows, value_rows, key_cols, value_cols, key_grad, value_grad, near_flat, sem = refs
    step = pl.program_id(0)
    load = pltpu.make_async_copy(weight, held, sem)
    chunks = items.shape[0]
    key_chunks = key_rows.shape[0] // LANES
    att_scale = 1.0 / math.sqrt(head_size)
    exponent_scale = att_scale * math.log2(math.e)
    pad = value_rows.shape[1] - head_size

    @pl.when(step == 0)
    def _():
        load.start()
        for s in range(key_chunks):
            if split:
                pair = pairs[s].astype(F32)
            else:
                pair = items[s].astype(F32)[head_size : 3 * head_size]
            at = slice(s * LANES, (s + 1) * LANES)
            keys, values = pair[:head_size], pair[head_size:]
            key_cols[:, at] = keys.astype(BF16)
            value_cols[:, at] = values.astype(BF16)
            key_rows[at, :] = keys.T.astype(BF16)
            value_rows[at, :] = jnp.concatenate(
                [values, jnp.ones((pad, LANES), F32)], axis=0
            ).T.astype(BF16)
        key_grad[...] = jnp.zeros_like(key_grad)
        value_grad[...] = jnp.zeros_like(value_grad)

    block = [items[step * group + g].astype(F32) for g in range(group)]
    queries = jnp.concatenate([b[:head_size] for b in block], axis=1)
    grads = jnp.concatenate([b[3 * head_size :] for b in block], axis=1)
    scores = jnp.dot(key_rows[...], queries.astype(BF16), preferred_element_type=F32)
    row_max = jnp.max(scores, axis=0, keepdims=True)
    exponent = jnp.exp2((scores - row_max) * exponent_scale)
    total = jnp.sum(exponent, axis=0, keepdims=True)
    weights = (exponent * (1.0 / total)).astype(BF16)
    attended = (
        jnp.dot(value_cols[...], weights, preferred_element_type=F32).astype(BF16).astype(F32)
    )
    less = -jnp.sum(attended * grads, axis=0, keepdims=True)
    less_high = less.astype(BF16).astype(F32)
    less_mid = (less - less_high).astype(BF16).astype(F32)
    less_low = less - less_high - less_mid
    place = lax.broadcasted_iota(jnp.int32, (pad, less.shape[1]), 0)
    tail = jnp.where(
        place == 0, less_high, jnp.where(place == 1, less_mid, jnp.where(place == 2, less_low, 0.0))
    )
    centred_grad = jnp.dot(
        value_rows[...],
        jnp.concatenate([grads, tail], axis=0).astype(BF16),
        preferred_element_type=F32,
    )
    score_grad = (weights.astype(F32) * centred_grad * att_scale).astype(BF16)
    query_grad = jnp.dot(key_cols[...], score_grad, preferred_element_type=F32)
    key_grad[...] += jnp.dot(score_grad, queries.T.astype(BF16), preferred_element_type=F32)
    value_grad[...] += jnp.dot(weights, grads.T.astype(BF16), preferred_element_type=F32)
    for g in range(group):
        at = slice(g * LANES, (g + 1) * LANES)
        near_flat[step * group + g] = jnp.concatenate(
            [attended[:, at], query_grad[:, at]], axis=0
        )

    @pl.when(step == pl.num_programs(0) - 1)
    def _():
        for s in range(key_chunks):
            at = slice(s * LANES, (s + 1) * LANES)
            grads_of = jnp.concatenate([key_grad[at, :].T, value_grad[at, :].T], axis=0)
            if split:
                far[s] = grads_of
            else:
                near[s] = jnp.concatenate([near_flat[s], grads_of], axis=0).astype(BF16)
        if split:
            near[...] = near_flat[...].astype(BF16)
        load.wait()


def attend(items, weight, pairs=None):
    chunks = items.shape[0]
    head_size = items.shape[1] // 4
    split = pairs is not None
    key_chunks = pairs.shape[0] if split else chunks
    key_len = key_chunks * LANES
    group = math.gcd(chunks, max(1, SCORE_LIMIT // (key_len * LANES)))
    pad = 8
    whole = lambda shape: pl.BlockSpec(shape, lambda i: (0,) * len(shape))
    if split:
        shapes = [
            jax.ShapeDtypeStruct((chunks, 2 * head_size, LANES), BF16),
            jax.ShapeDtypeStruct((key_chunks, 2 * head_size, LANES), F32),
        ]
        operands = (items, weight, pairs)
    else:
        shapes = [jax.ShapeDtypeStruct((chunks, 4 * head_size, LANES), BF16)]
        operands = (items, weight)
    specs = [whole(x.shape) for x in operands]
    specs[1] = pl.BlockSpec(memory_space=pl.ANY)
    shapes = [jax.ShapeDtypeStruct(weight.shape, weight.dtype)] + shapes
    return pl.pallas_call(
        functools.partial(attend_kernel, head_size, group, split),
        grid=(chunks // group,),
        in_specs=specs,
        out_specs=[pl.BlockSpec(memory_space=pltpu.VMEM)] + [whole(x.shape) for x in shapes[1:]],
        out_shape=shapes,
        scratch_shapes=[
            pltpu.VMEM((key_len, head_size), BF16),
            pltpu.VMEM((key_len, head_size + pad), BF16),
            pltpu.VMEM((head_size, key_len), BF16),
            pltpu.VMEM((head_size, key_len), BF16),
            pltpu.VMEM((key_len, head_size), F32),
            pltpu.VMEM((key_len, head_size), F32),
            pltpu.VMEM((chunks, 2 * head_size, LANES), F32),
            pltpu.SemaphoreType.DMA,
        ],
        compiler_params=params(ATTEND_LIMIT),
        name="attend",
    )(*operands)


def finish_kernel(
    head_size, items, tokens, scale, gate, qkv_w, out_w, cot,
    block_output, grad_input, sums, grad_cols,
):
    width = tokens.shape[1]
    flat = [items[head].astype(F32) for head in range(H)]
    for part in range(3):
        grad_cols[part * width : (part + 1) * width, :] = jnp.concatenate(
            [x[(part + 1) * head_size : (part + 2) * head_size] for x in flat], axis=0
        ).astype(BF16)
    att = jnp.concatenate([x[:head_size] for x in flat], axis=0).T.astype(BF16)
    out = jnp.dot(att, out_w[...], preferred_element_type=F32)
    back = jnp.dot(qkv_w[...], grad_cols[...], preferred_element_type=F32).T
    wide, normed, inv_std = normalise(tokens[...])
    cot_wide = cot[...].astype(F32)
    block_output[...] = (wide + row(gate) * out).astype(BF16)
    sums[...] = jnp.concatenate(
        [
            jnp.sum(back, axis=0, keepdims=True),
            jnp.sum(back * normed, axis=0, keepdims=True),
            jnp.sum(cot_wide * out, axis=0, keepdims=True),
        ],
        axis=0,
    )
    normed_grad = back * (1.0 + row(scale))
    first_mean = jnp.mean(normed_grad, axis=1, keepdims=True)
    second_mean = jnp.mean(normed_grad * normed, axis=1, keepdims=True)
    grad_input[...] = (
        cot_wide + inv_std * (normed_grad - first_mean - normed * second_mean)
    ).astype(BF16)


def finish(items, tokens, scale, gate, qkv_w, out_w, cot):
    tok_rows, width = tokens.shape
    head_size = width // H
    vmem = pl.BlockSpec(memory_space=pltpu.VMEM)
    return pl.pallas_call(
        functools.partial(finish_kernel, head_size),
        in_specs=[vmem] * 7,
        out_specs=[vmem] * 3,
        out_shape=[
            jax.ShapeDtypeStruct((tok_rows, width), BF16),
            jax.ShapeDtypeStruct((tok_rows, width), BF16),
            jax.ShapeDtypeStruct((3, width), F32),
        ],
        scratch_shapes=[pltpu.VMEM((3 * width, tok_rows), BF16)],
        compiler_params=pltpu.CompilerParams(vmem_limit_bytes=FINISH_LIMIT),
        name="finish",
    )(items, tokens, scale, gate, qkv_w, out_w, cot)


def from_partner(shard, axis, stride):
    return lax.ppermute(shard, axis, [(i, i ^ stride) for i in range(lax.axis_size(axis))])


def exchange(blocks):
    return lax.all_to_all(blocks, "seq", split_axis=0, concat_axis=0, tiled=True)


def per_device(tokens, shift_cond, scale_cond, gate_cond, qkv_weight, out_weight, cotangent):
    seq_count = lax.axis_size("seq")
    repeat = seq_count // H
    levels = repeat.bit_length() - 1
    tok_rows, width = tokens.shape
    head_size = width // H
    sub_rows = tok_rows // repeat
    packed = project(tokens, shift_cond, scale_cond, gate_cond, qkv_weight, out_weight, cotangent)
    if repeat == 1:
        held, made = attend(exchange(packed), qkv_weight)
        returned = exchange(made)
    else:
        packed = packed.reshape(H, 4 * head_size, repeat, sub_rows).transpose(0, 2, 1, 3)
        landed = exchange(packed.reshape(seq_count, 4 * head_size, sub_rows))
        items = landed.reshape(H, repeat, 4 * head_size, sub_rows).transpose(0, 2, 1, 3)
        items = items.reshape(H, 4 * head_size, tok_rows)
        pairs = items[:, head_size : 3 * head_size]
        for level in range(levels):
            pairs = jnp.concatenate([pairs, from_partner(pairs, "seq", 1 << level)], axis=0)
        held, near, far = attend(items, qkv_weight, pairs)
        for level in reversed(range(levels)):
            middle = far.shape[0] // 2
            far = far[:middle] + from_partner(far[middle:], "seq", 1 << level)
        made = jnp.concatenate([near, far.astype(BF16)], axis=1)
        made = made.reshape(H, 4 * head_size, repeat, sub_rows).transpose(0, 2, 1, 3)
        back = exchange(made.reshape(seq_count, 4 * head_size, sub_rows))
        returned = back.reshape(H, repeat, 4 * head_size, sub_rows).transpose(0, 2, 1, 3)
        returned = returned.reshape(H, 4 * head_size, tok_rows)
    block_output, grad_input, sums = finish(
        returned, tokens, scale_cond, gate_cond, held, out_weight, cotangent
    )
    stride = 1
    while stride < seq_count:
        sums = sums + from_partner(sums, "seq", stride)
        stride *= 2
    grad_condition = sums / math.sqrt(tok_rows * seq_count)
    return (block_output, grad_input, grad_condition)


def solution(mesh):
    return jax.shard_map(
        per_device,
        mesh=mesh,
        in_specs=(
            P(("groups", "seq"), None),
            P("groups"),
            P("groups"),
            P("groups"),
            P(),
            P(),
            P(("groups", "seq"), None),
        ),
        out_specs=(P(("groups", "seq"), None), P(("groups", "seq"), None), P("groups", None)),
        check_vma=False,
    )
```

```python
import functools
import math

import jax
import jax.numpy as jnp
from jax import lax
from jax.experimental import pallas as pl
from jax.experimental.pallas import tpu as pltpu
from jax.sharding import PartitionSpec as P

H = 16
LANES = 128
SCORE_LIMIT = 2048 * 2048
F32 = jnp.float32
BF16 = jnp.bfloat16
PROJECT_LIMIT = 60 * 1024 * 1024
ATTEND_LIMIT = 44 * 1024 * 1024
FINISH_LIMIT = 24 * 1024 * 1024


def params(limit):
    return pltpu.CompilerParams(dimension_semantics=("arbitrary",), vmem_limit_bytes=limit)


def row(vector):
    return vector[...].reshape(1, vector.shape[0])


def normalise(tokens):
    wide = tokens.astype(F32)
    row_mean = jnp.mean(wide, axis=1, keepdims=True)
    centered = wide - row_mean
    variance = jnp.mean(centered * centered, axis=1, keepdims=True)
    inv_std = lax.rsqrt(variance + 1e-06)
    return wide, centered * inv_std, inv_std


def project_kernel(head_size, *refs):
    sources, out, held, sems, packed = refs[:7], refs[7], refs[8:15], refs[15], refs[16]
    tokens, shift, scale, gate, cot, out_w, qkv_w = held
    width = tokens.shape[1]
    copies = [
        pltpu.make_async_copy(source, target, sems.at[i])
        for i, (source, target) in enumerate(zip(sources[:6], held[:6]))
    ]
    parts = [slice(part * width, (part + 1) * width) for part in range(3)]
    copies += [
        pltpu.make_async_copy(sources[6].at[:, at], qkv_w.at[:, at], sems.at[6 + part])
        for part, at in enumerate(parts)
    ]
    for copy in copies:
        copy.start()
    for copy in copies[:5]:
        copy.wait()
    _, normed, _ = normalise(tokens[...])
    modulated = (normed * (1.0 + row(scale)) + row(shift)).astype(BF16)
    gated = (row(gate) * cot[...].astype(F32)).astype(BF16)
    copies[5].wait()
    pulled = lax.dot_general(
        out_w[...], gated, (((1,), (1,)), ((), ())), preferred_element_type=F32
    )

    def part_of(part):
        copies[6 + part].wait()
        return jnp.dot(modulated, qkv_w[:, parts[part]], preferred_element_type=F32).T

    def send(first, second, half):
        rows = slice(half * 2 * head_size, (half + 1) * 2 * head_size)
        for head in range(H):
            at = slice(head * head_size, (head + 1) * head_size)
            packed[head, rows, :] = jnp.concatenate([first[at], second[at]], axis=0).astype(BF16)
        copy = pltpu.make_async_copy(packed.at[:, rows, :], out.at[:, rows, :], sems.at[9 + half])
        copy.start()
        return copy

    leaving = [send(part_of(0), part_of(1), 0)]
    leaving.append(send(part_of(2), pulled, 1))
    for copy in leaving:
        copy.wait()


def project(tokens, shift, scale, gate, qkv_w, out_w, cot):
    tok_rows, width = tokens.shape
    head_size = width // H
    operands = (tokens, shift, scale, gate, cot, out_w, qkv_w)
    hbm = pl.BlockSpec(memory_space=pl.ANY)
    packed = (H, 4 * head_size, tok_rows)
    return pl.pallas_call(
        functools.partial(project_kernel, head_size),
        in_specs=[hbm] * 7,
        out_specs=hbm,
        out_shape=jax.ShapeDtypeStruct(packed, BF16),
        scratch_shapes=[pltpu.VMEM(x.shape, x.dtype) for x in operands]
        + [pltpu.SemaphoreType.DMA((11,)), pltpu.VMEM(packed, BF16)],
        compiler_params=pltpu.CompilerParams(vmem_limit_bytes=PROJECT_LIMIT),
        name="project",
    )(*operands)


def attend_kernel(head_size, group, split, items, weight, *refs):
    if split:
        pairs, held, near, far = refs[:4]
        refs = refs[4:]
    else:
        held, near = refs[:2]
        refs = refs[2:]
    key_rows, value_rows, key_cols, value_cols, key_grad, value_grad, near_flat, sem = refs
    step = pl.program_id(0)
    load = pltpu.make_async_copy(weight, held, sem)
    chunks = items.shape[0]
    key_chunks = key_rows.shape[0] // LANES
    att_scale = 1.0 / math.sqrt(head_size)
    exponent_scale = att_scale * math.log2(math.e)
    pad = value_rows.shape[1] - head_size

    @pl.when(step == 0)
    def _():
        load.start()
        for s in range(key_chunks):
            if split:
                pair = pairs[s].astype(F32)
            else:
                pair = items[s].astype(F32)[head_size : 3 * head_size]
            at = slice(s * LANES, (s + 1) * LANES)
            keys, values = pair[:head_size], pair[head_size:]
            key_cols[:, at] = keys.astype(BF16)
            value_cols[:, at] = values.astype(BF16)
            key_rows[at, :] = keys.T.astype(BF16)
            value_rows[at, :] = jnp.concatenate(
                [values, jnp.ones((pad, LANES), F32)], axis=0
            ).T.astype(BF16)
        key_grad[...] = jnp.zeros_like(key_grad)
        value_grad[...] = jnp.zeros_like(value_grad)

    block = [items[step * group + g].astype(F32) for g in range(group)]
    queries = jnp.concatenate([b[:head_size] for b in block], axis=1)
    grads = jnp.concatenate([b[3 * head_size :] for b in block], axis=1)
    scores = jnp.dot(key_rows[...], queries.astype(BF16), preferred_element_type=F32)
    row_max = jnp.max(scores, axis=0, keepdims=True)
    exponent = jnp.exp2((scores - row_max) * exponent_scale)
    total = jnp.sum(exponent, axis=0, keepdims=True)
    weights = (exponent * (1.0 / total)).astype(BF16)
    attended = (
        jnp.dot(value_cols[...], weights, preferred_element_type=F32).astype(BF16).astype(F32)
    )
    less = -jnp.sum(attended * grads, axis=0, keepdims=True)
    less_high = less.astype(BF16).astype(F32)
    less_mid = (less - less_high).astype(BF16).astype(F32)
    less_low = less - less_high - less_mid
    place = lax.broadcasted_iota(jnp.int32, (pad, less.shape[1]), 0)
    tail = jnp.where(
        place == 0, less_high, jnp.where(place == 1, less_mid, jnp.where(place == 2, less_low, 0.0))
    )
    centred_grad = jnp.dot(
        value_rows[...],
        jnp.concatenate([grads, tail], axis=0).astype(BF16),
        preferred_element_type=F32,
    )
    score_grad = (weights.astype(F32) * centred_grad * att_scale).astype(BF16)
    query_grad = jnp.dot(key_cols[...], score_grad, preferred_element_type=F32)
    key_grad[...] += jnp.dot(score_grad, queries.T.astype(BF16), preferred_element_type=F32)
    value_grad[...] += jnp.dot(weights, grads.T.astype(BF16), preferred_element_type=F32)
    for g in range(group):
        at = slice(g * LANES, (g + 1) * LANES)
        near_flat[step * group + g] = jnp.concatenate(
            [attended[:, at], query_grad[:, at]], axis=0
        )

    @pl.when(step == pl.num_programs(0) - 1)
    def _():
        for s in range(key_chunks):
            at = slice(s * LANES, (s + 1) * LANES)
            grads_of = jnp.concatenate([key_grad[at, :].T, value_grad[at, :].T], axis=0)
            if split:
                far[s] = grads_of
            else:
                near[s] = jnp.concatenate([near_flat[s], grads_of], axis=0).astype(BF16)
        if split:
            near[...] = near_flat[...].astype(BF16)
        load.wait()


def attend(items, weight, pairs=None):
    chunks = items.shape[0]
    head_size = items.shape[1] // 4
    split = pairs is not None
    key_chunks = pairs.shape[0] if split else chunks
    key_len = key_chunks * LANES
    group = math.gcd(chunks, max(1, SCORE_LIMIT // (key_len * LANES)))
    pad = 8
    whole = lambda shape: pl.BlockSpec(shape, lambda i: (0,) * len(shape))
    if split:
        shapes = [
            jax.ShapeDtypeStruct((chunks, 2 * head_size, LANES), BF16),
            jax.ShapeDtypeStruct((key_chunks, 2 * head_size, LANES), F32),
        ]
        operands = (items, weight, pairs)
    else:
        shapes = [jax.ShapeDtypeStruct((chunks, 4 * head_size, LANES), BF16)]
        operands = (items, weight)
    specs = [whole(x.shape) for x in operands]
    specs[1] = pl.BlockSpec(memory_space=pl.ANY)
    shapes = [jax.ShapeDtypeStruct(weight.shape, weight.dtype)] + shapes
    return pl.pallas_call(
        functools.partial(attend_kernel, head_size, group, split),
        grid=(chunks // group,),
        in_specs=specs,
        out_specs=[pl.BlockSpec(memory_space=pltpu.VMEM)] + [whole(x.shape) for x in shapes[1:]],
        out_shape=shapes,
        scratch_shapes=[
            pltpu.VMEM((key_len, head_size), BF16),
            pltpu.VMEM((key_len, head_size + pad), BF16),
            pltpu.VMEM((head_size, key_len), BF16),
            pltpu.VMEM((head_size, key_len), BF16),
            pltpu.VMEM((key_len, head_size), F32),
            pltpu.VMEM((key_len, head_size), F32),
            pltpu.VMEM((chunks, 2 * head_size, LANES), F32),
            pltpu.SemaphoreType.DMA,
        ],
        compiler_params=params(ATTEND_LIMIT),
        name="attend",
    )(*operands)


def gather_kernel(
    head_size, items, tokens, qkv_w, out_w, cot, branch, mod_grad, sums, grad_cols
):
    width = tokens.shape[1]
    flat = [items[head].astype(F32) for head in range(H)]
    for part in range(3):
        grad_cols[part * width : (part + 1) * width, :] = jnp.concatenate(
            [x[(part + 1) * head_size : (part + 2) * head_size] for x in flat], axis=0
        ).astype(BF16)
    att = jnp.concatenate([x[:head_size] for x in flat], axis=0).T.astype(BF16)
    out = jnp.dot(att, out_w[...], preferred_element_type=F32)
    back = jnp.dot(qkv_w[...], grad_cols[...], preferred_element_type=F32).T
    _, normed, _ = normalise(tokens[...])
    branch[...] = out
    mod_grad[...] = back
    sums[...] = jnp.concatenate(
        [
            jnp.sum(back, axis=0, keepdims=True),
            jnp.sum(back * normed, axis=0, keepdims=True),
            jnp.sum(cot[...].astype(F32) * out, axis=0, keepdims=True),
        ],
        axis=0,
    )


def gather(items, tokens, qkv_w, out_w, cot):
    tok_rows, width = tokens.shape
    vmem = pl.BlockSpec(memory_space=pltpu.VMEM)
    return pl.pallas_call(
        functools.partial(gather_kernel, width // H),
        in_specs=[vmem] * 5,
        out_specs=[vmem] * 3,
        out_shape=[
            jax.ShapeDtypeStruct((tok_rows, width), F32),
            jax.ShapeDtypeStruct((tok_rows, width), F32),
            jax.ShapeDtypeStruct((3, width), F32),
        ],
        scratch_shapes=[pltpu.VMEM((3 * width, tok_rows), BF16)],
        compiler_params=pltpu.CompilerParams(vmem_limit_bytes=FINISH_LIMIT),
        name="gather",
    )(items, tokens, qkv_w, out_w, cot)


def finish_kernel(branch, mod_grad, tokens, scale, gate, cot, block_output, grad_input):
    wide, normed, inv_std = normalise(tokens[...])
    block_output[...] = (wide + row(gate) * branch[...]).astype(BF16)
    normed_grad = mod_grad[...] * (1.0 + row(scale))
    first_mean = jnp.mean(normed_grad, axis=1, keepdims=True)
    second_mean = jnp.mean(normed_grad * normed, axis=1, keepdims=True)
    grad_input[...] = (
        cot[...].astype(F32) + inv_std * (normed_grad - first_mean - normed * second_mean)
    ).astype(BF16)


def finish(branch, mod_grad, tokens, scale, gate, cot):
    vmem = pl.BlockSpec(memory_space=pltpu.VMEM)
    return pl.pallas_call(
        finish_kernel,
        in_specs=[vmem] * 6,
        out_specs=[vmem] * 2,
        out_shape=[jax.ShapeDtypeStruct(tokens.shape, BF16)] * 2,
        compiler_params=pltpu.CompilerParams(vmem_limit_bytes=FINISH_LIMIT),
        cost_estimate=pl.CostEstimate(
            flops=30 * tokens.size, transcendentals=0, bytes_accessed=16 * tokens.size
        ),
        name="finish",
    )(branch, mod_grad, tokens, scale, gate, cot)


def from_partner(shard, axis, stride):
    return lax.ppermute(shard, axis, [(i, i ^ stride) for i in range(lax.axis_size(axis))])


def exchange(blocks):
    return lax.all_to_all(blocks, "seq", split_axis=0, concat_axis=0, tiled=True)


def per_device(tokens, shift_cond, scale_cond, gate_cond, qkv_weight, out_weight, cotangent):
    seq_count = lax.axis_size("seq")
    repeat = seq_count // H
    levels = repeat.bit_length() - 1
    tok_rows, width = tokens.shape
    head_size = width // H
    sub_rows = tok_rows // repeat
    packed = project(tokens, shift_cond, scale_cond, gate_cond, qkv_weight, out_weight, cotangent)
    if repeat == 1:
        held, made = attend(exchange(packed), qkv_weight)
        returned = exchange(made)
    else:
        packed = packed.reshape(H, 4 * head_size, repeat, sub_rows).transpose(0, 2, 1, 3)
        landed = exchange(packed.reshape(seq_count, 4 * head_size, sub_rows))
        items = landed.reshape(H, repeat, 4 * head_size, sub_rows).transpose(0, 2, 1, 3)
        items = items.reshape(H, 4 * head_size, tok_rows)
        pairs = items[:, head_size : 3 * head_size]
        for level in range(levels):
            pairs = jnp.concatenate([pairs, from_partner(pairs, "seq", 1 << level)], axis=0)
        held, near, far = attend(items, qkv_weight, pairs)
        for level in reversed(range(levels)):
            middle = far.shape[0] // 2
            far = far[:middle] + from_partner(far[middle:], "seq", 1 << level)
        made = jnp.concatenate([near, far.astype(BF16)], axis=1)
        made = made.reshape(H, 4 * head_size, repeat, sub_rows).transpose(0, 2, 1, 3)
        back = exchange(made.reshape(seq_count, 4 * head_size, sub_rows))
        returned = back.reshape(H, repeat, 4 * head_size, sub_rows).transpose(0, 2, 1, 3)
        returned = returned.reshape(H, 4 * head_size, tok_rows)
    branch, mod_grad, sums = gather(returned, tokens, held, out_weight, cotangent)
    block_output, grad_input = finish(
        branch, mod_grad, tokens, scale_cond, gate_cond, cotangent
    )
    stride = 1
    while stride < seq_count:
        sums = sums + from_partner(sums, "seq", stride)
        stride *= 2
    return (block_output, grad_input, sums / math.sqrt(tok_rows * seq_count))


def solution(mesh):
    return jax.shard_map(
        per_device,
        mesh=mesh,
        in_specs=(
            P(("groups", "seq"), None),
            P("groups"),
            P("groups"),
            P("groups"),
            P(),
            P(),
            P(("groups", "seq"), None),
        ),
        out_specs=(P(("groups", "seq"), None), P(("groups", "seq"), None), P("groups", None)),
        check_vma=False,
    )
```

```python
import functools
import math

import jax
import jax.numpy as jnp
from jax import lax
from jax.experimental import pallas as pl
from jax.experimental.pallas import tpu as pltpu
from jax.sharding import PartitionSpec as P

H = 16
LANES = 128
SCORE_LIMIT = 2048 * 2048
F32 = jnp.float32
BF16 = jnp.bfloat16
PROJECT_LIMIT = 60 * 1024 * 1024
ATTEND_LIMIT = 44 * 1024 * 1024
FINISH_LIMIT = 24 * 1024 * 1024


def params(limit):
    return pltpu.CompilerParams(dimension_semantics=("arbitrary",), vmem_limit_bytes=limit)


def row(vector):
    return vector[...].reshape(1, vector.shape[0])


def normalise(tokens):
    wide = tokens.astype(F32)
    row_mean = jnp.mean(wide, axis=1, keepdims=True)
    centered = wide - row_mean
    variance = jnp.mean(centered * centered, axis=1, keepdims=True)
    inv_std = lax.rsqrt(variance + 1e-06)
    return wide, centered * inv_std, inv_std


def project_kernel(head_size, *refs):
    sources, out, held, sems, packed = refs[:7], refs[7], refs[8:15], refs[15], refs[16]
    tokens, shift, scale, gate, cot, out_w, qkv_w = held
    width = tokens.shape[1]
    copies = [
        pltpu.make_async_copy(source, target, sems.at[i])
        for i, (source, target) in enumerate(zip(sources[:6], held[:6]))
    ]
    parts = [slice(part * width, (part + 1) * width) for part in range(3)]
    copies += [
        pltpu.make_async_copy(sources[6].at[:, at], qkv_w.at[:, at], sems.at[6 + part])
        for part, at in enumerate(parts)
    ]
    for copy in copies:
        copy.start()
    for copy in copies[:5]:
        copy.wait()
    _, normed, _ = normalise(tokens[...])
    modulated = (normed * (1.0 + row(scale)) + row(shift)).astype(BF16)
    gated = (row(gate) * cot[...].astype(F32)).astype(BF16)
    copies[5].wait()
    pulled = lax.dot_general(
        out_w[...], gated, (((1,), (1,)), ((), ())), preferred_element_type=F32
    )

    def part_of(part):
        copies[6 + part].wait()
        return jnp.dot(modulated, qkv_w[:, parts[part]], preferred_element_type=F32).T

    def send(first, second, half):
        rows = slice(half * 2 * head_size, (half + 1) * 2 * head_size)
        for head in range(H):
            at = slice(head * head_size, (head + 1) * head_size)
            packed[head, rows, :] = jnp.concatenate([first[at], second[at]], axis=0).astype(BF16)
        copy = pltpu.make_async_copy(packed.at[:, rows, :], out.at[:, rows, :], sems.at[9 + half])
        copy.start()
        return copy

    leaving = [send(part_of(0), part_of(1), 0)]
    leaving.append(send(part_of(2), pulled, 1))
    for copy in leaving:
        copy.wait()


def project(tokens, shift, scale, gate, qkv_w, out_w, cot):
    tok_rows, width = tokens.shape
    head_size = width // H
    operands = (tokens, shift, scale, gate, cot, out_w, qkv_w)
    hbm = pl.BlockSpec(memory_space=pl.ANY)
    packed = (H, 4 * head_size, tok_rows)
    return pl.pallas_call(
        functools.partial(project_kernel, head_size),
        in_specs=[hbm] * 7,
        out_specs=hbm,
        out_shape=jax.ShapeDtypeStruct(packed, BF16),
        scratch_shapes=[pltpu.VMEM(x.shape, x.dtype) for x in operands]
        + [pltpu.SemaphoreType.DMA((11,)), pltpu.VMEM(packed, BF16)],
        compiler_params=pltpu.CompilerParams(vmem_limit_bytes=PROJECT_LIMIT),
        name="project",
    )(*operands)


def attend_kernel(head_size, group, split, items, weight, *refs):
    if split:
        pairs, held, near, far = refs[:4]
        refs = refs[4:]
    else:
        held, near = refs[:2]
        refs = refs[2:]
    key_rows, value_rows, key_cols, value_cols, key_grad, value_grad, near_flat, sem = refs
    step = pl.program_id(0)
    load = pltpu.make_async_copy(weight, held, sem)
    chunks = items.shape[0]
    key_chunks = key_rows.shape[0] // LANES
    att_scale = 1.0 / math.sqrt(head_size)
    exponent_scale = att_scale * math.log2(math.e)
    pad = value_rows.shape[1] - head_size

    @pl.when(step == 0)
    def _():
        load.start()
        for s in range(key_chunks):
            if split:
                pair = pairs[s].astype(F32)
            else:
                pair = items[s].astype(F32)[head_size : 3 * head_size]
            at = slice(s * LANES, (s + 1) * LANES)
            keys, values = pair[:head_size], pair[head_size:]
            key_cols[:, at] = keys.astype(BF16)
            value_cols[:, at] = values.astype(BF16)
            key_rows[at, :] = keys.T.astype(BF16)
            value_rows[at, :] = jnp.concatenate(
                [values, jnp.ones((pad, LANES), F32)], axis=0
            ).T.astype(BF16)
        key_grad[...] = jnp.zeros_like(key_grad)
        value_grad[...] = jnp.zeros_like(value_grad)

    block = [items[step * group + g].astype(F32) for g in range(group)]
    queries = jnp.concatenate([b[:head_size] for b in block], axis=1)
    grads = jnp.concatenate([b[3 * head_size :] for b in block], axis=1)
    scores = jnp.dot(key_rows[...], queries.astype(BF16), preferred_element_type=F32)
    row_max = jnp.max(scores, axis=0, keepdims=True)
    exponent = jnp.exp2((scores - row_max) * exponent_scale)
    total = jnp.sum(exponent, axis=0, keepdims=True)
    weights = (exponent * (1.0 / total)).astype(BF16)
    attended = (
        jnp.dot(value_cols[...], weights, preferred_element_type=F32).astype(BF16).astype(F32)
    )
    less = -jnp.sum(attended * grads, axis=0, keepdims=True)
    less_high = less.astype(BF16).astype(F32)
    less_mid = (less - less_high).astype(BF16).astype(F32)
    less_low = less - less_high - less_mid
    place = lax.broadcasted_iota(jnp.int32, (pad, less.shape[1]), 0)
    tail = jnp.where(
        place == 0, less_high, jnp.where(place == 1, less_mid, jnp.where(place == 2, less_low, 0.0))
    )
    centred_grad = jnp.dot(
        value_rows[...],
        jnp.concatenate([grads, tail], axis=0).astype(BF16),
        preferred_element_type=F32,
    )
    score_grad = (weights.astype(F32) * centred_grad * att_scale).astype(BF16)
    query_grad = jnp.dot(key_cols[...], score_grad, preferred_element_type=F32)
    key_grad[...] += jnp.dot(score_grad, queries.T.astype(BF16), preferred_element_type=F32)
    value_grad[...] += jnp.dot(weights, grads.T.astype(BF16), preferred_element_type=F32)
    for g in range(group):
        at = slice(g * LANES, (g + 1) * LANES)
        near_flat[step * group + g] = jnp.concatenate(
            [attended[:, at], query_grad[:, at]], axis=0
        )

    @pl.when(step == pl.num_programs(0) - 1)
    def _():
        for s in range(key_chunks):
            at = slice(s * LANES, (s + 1) * LANES)
            grads_of = jnp.concatenate([key_grad[at, :].T, value_grad[at, :].T], axis=0)
            if split:
                far[s] = grads_of
            else:
                near[s] = jnp.concatenate([near_flat[s], grads_of], axis=0).astype(BF16)
        if split:
            near[...] = near_flat[...].astype(BF16)
        load.wait()


def attend(items, weight, pairs=None):
    chunks = items.shape[0]
    head_size = items.shape[1] // 4
    split = pairs is not None
    key_chunks = pairs.shape[0] if split else chunks
    key_len = key_chunks * LANES
    group = math.gcd(chunks, max(1, SCORE_LIMIT // (key_len * LANES)))
    pad = 8
    whole = lambda shape: pl.BlockSpec(shape, lambda i: (0,) * len(shape))
    if split:
        shapes = [
            jax.ShapeDtypeStruct((chunks, 2 * head_size, LANES), BF16),
            jax.ShapeDtypeStruct((key_chunks, 2 * head_size, LANES), F32),
        ]
        operands = (items, weight, pairs)
    else:
        shapes = [jax.ShapeDtypeStruct((chunks, 4 * head_size, LANES), BF16)]
        operands = (items, weight)
    specs = [whole(x.shape) for x in operands]
    specs[1] = pl.BlockSpec(memory_space=pl.ANY)
    shapes = [jax.ShapeDtypeStruct(weight.shape, weight.dtype)] + shapes
    return pl.pallas_call(
        functools.partial(attend_kernel, head_size, group, split),
        grid=(chunks // group,),
        in_specs=specs,
        out_specs=[pl.BlockSpec(memory_space=pltpu.VMEM)] + [whole(x.shape) for x in shapes[1:]],
        out_shape=shapes,
        scratch_shapes=[
            pltpu.VMEM((key_len, head_size), BF16),
            pltpu.VMEM((key_len, head_size + pad), BF16),
            pltpu.VMEM((head_size, key_len), BF16),
            pltpu.VMEM((head_size, key_len), BF16),
            pltpu.VMEM((key_len, head_size), F32),
            pltpu.VMEM((key_len, head_size), F32),
            pltpu.VMEM((chunks, 2 * head_size, LANES), F32),
            pltpu.SemaphoreType.DMA,
        ],
        compiler_params=params(ATTEND_LIMIT),
        name="attend",
    )(*operands)


def gather_kernel(
    head_size, items, tokens, qkv_w, out_w, cot, branch, mod_grad, sums, grad_cols
):
    width = tokens.shape[1]
    flat = [items[head].astype(F32) for head in range(H)]
    for part in range(3):
        grad_cols[part * width : (part + 1) * width, :] = jnp.concatenate(
            [x[(part + 1) * head_size : (part + 2) * head_size] for x in flat], axis=0
        ).astype(BF16)
    att = jnp.concatenate([x[:head_size] for x in flat], axis=0).T.astype(BF16)
    out = jnp.dot(att, out_w[...], preferred_element_type=F32)
    back = jnp.dot(qkv_w[...], grad_cols[...], preferred_element_type=F32).T
    _, normed, _ = normalise(tokens[...])
    branch[...] = out
    mod_grad[...] = back
    sums[...] = jnp.concatenate(
        [
            jnp.sum(back, axis=0, keepdims=True),
            jnp.sum(back * normed, axis=0, keepdims=True),
            jnp.sum(cot[...].astype(F32) * out, axis=0, keepdims=True),
        ],
        axis=0,
    )


def gather(items, tokens, qkv_w, out_w, cot):
    tok_rows, width = tokens.shape
    vmem = pl.BlockSpec(memory_space=pltpu.VMEM)
    return pl.pallas_call(
        functools.partial(gather_kernel, width // H),
        in_specs=[vmem] * 5,
        out_specs=[vmem] * 3,
        out_shape=[
            jax.ShapeDtypeStruct((tok_rows, width), F32),
            jax.ShapeDtypeStruct((tok_rows, width), F32),
            jax.ShapeDtypeStruct((3, width), F32),
        ],
        scratch_shapes=[pltpu.VMEM((3 * width, tok_rows), BF16)],
        compiler_params=pltpu.CompilerParams(vmem_limit_bytes=FINISH_LIMIT),
        name="gather",
    )(items, tokens, qkv_w, out_w, cot)


def finish_kernel(branch, mod_grad, tokens, scale, gate, cot, block_output, grad_input):
    wide, normed, inv_std = normalise(tokens[...])
    block_output[...] = (wide + row(gate) * branch[...]).astype(BF16)
    normed_grad = mod_grad[...] * (1.0 + row(scale))
    first_mean = jnp.mean(normed_grad, axis=1, keepdims=True)
    second_mean = jnp.mean(normed_grad * normed, axis=1, keepdims=True)
    grad_input[...] = (
        cot[...].astype(F32) + inv_std * (normed_grad - first_mean - normed * second_mean)
    ).astype(BF16)


def finish(branch, mod_grad, tokens, scale, gate, cot):
    vmem = pl.BlockSpec(memory_space=pltpu.VMEM)
    return pl.pallas_call(
        finish_kernel,
        in_specs=[vmem] * 6,
        out_specs=[vmem] * 2,
        out_shape=[jax.ShapeDtypeStruct(tokens.shape, BF16)] * 2,
        compiler_params=pltpu.CompilerParams(vmem_limit_bytes=FINISH_LIMIT),
        cost_estimate=pl.CostEstimate(
            flops=30 * tokens.size, transcendentals=0, bytes_accessed=16 * tokens.size
        ),
        name="finish",
    )(branch, mod_grad, tokens, scale, gate, cot)


def from_partner(shard, axis, stride):
    return lax.ppermute(shard, axis, [(i, i ^ stride) for i in range(lax.axis_size(axis))])


def exchange(blocks):
    return lax.all_to_all(blocks, "seq", split_axis=0, concat_axis=0, tiled=True)


def per_device(tokens, shift_cond, scale_cond, gate_cond, qkv_weight, out_weight, cotangent):
    seq_count = lax.axis_size("seq")
    repeat = seq_count // H
    levels = repeat.bit_length() - 1
    tok_rows, width = tokens.shape
    head_size = width // H
    sub_rows = tok_rows // repeat
    packed = project(tokens, shift_cond, scale_cond, gate_cond, qkv_weight, out_weight, cotangent)
    if repeat == 1:
        held, made = attend(exchange(packed), qkv_weight)
        returned = exchange(made)
    else:
        packed = packed.reshape(H, 4 * head_size, repeat, sub_rows).transpose(0, 2, 1, 3)
        landed = exchange(packed.reshape(seq_count, 4 * head_size, sub_rows))
        items = landed.reshape(H, repeat, 4 * head_size, sub_rows).transpose(0, 2, 1, 3)
        items = items.reshape(H, 4 * head_size, tok_rows)
        pairs = items[:, head_size : 3 * head_size]
        for level in range(levels):
            pairs = jnp.concatenate([pairs, from_partner(pairs, "seq", 1 << level)], axis=0)
        held, near, far = attend(items, qkv_weight, pairs)
        for level in reversed(range(levels)):
            middle = far.shape[0] // 2
            far = far[:middle] + from_partner(far[middle:], "seq", 1 << level)
        made = jnp.concatenate([near, far.astype(BF16)], axis=1)
        made = made.reshape(H, 4 * head_size, repeat, sub_rows).transpose(0, 2, 1, 3)
        back = exchange(made.reshape(seq_count, 4 * head_size, sub_rows))
        returned = back.reshape(H, repeat, 4 * head_size, sub_rows).transpose(0, 2, 1, 3)
        returned = returned.reshape(H, 4 * head_size, tok_rows)
    branch, mod_grad, sums = gather(returned, tokens, held, out_weight, cotangent)
    block_output, grad_input = finish(
        branch, mod_grad, tokens, scale_cond, gate_cond, cotangent
    )
    stride = 1
    while stride < seq_count:
        if stride == 2 and seq_count >= 8:
            first, second, third = (from_partner(sums, "seq", k * stride) for k in (1, 2, 3))
            sums = (sums + first) + (second + third)
            stride *= 4
        else:
            sums = sums + from_partner(sums, "seq", stride)
            stride *= 2
    return (block_output, grad_input, sums / math.sqrt(tok_rows * seq_count))


def solution(mesh):
    return jax.shard_map(
        per_device,
        mesh=mesh,
        in_specs=(
            P(("groups", "seq"), None),
            P("groups"),
            P("groups"),
            P("groups"),
            P(),
            P(),
            P(("groups", "seq"), None),
        ),
        out_specs=(P(("groups", "seq"), None), P(("groups", "seq"), None), P("groups", None)),
        check_vma=False,
    )
```

```python
import functools
import math

import jax
import jax.numpy as jnp
from jax import lax
from jax.experimental import pallas as pl
from jax.experimental.pallas import tpu as pltpu
from jax.sharding import PartitionSpec as P

H = 16
LANES = 128
SCORE_LIMIT = 2048 * 2048
F32 = jnp.float32
BF16 = jnp.bfloat16
PROJECT_LIMIT = 60 * 1024 * 1024
ATTEND_LIMIT = 44 * 1024 * 1024
FINISH_LIMIT = 24 * 1024 * 1024


def params(limit):
    return pltpu.CompilerParams(dimension_semantics=("arbitrary",), vmem_limit_bytes=limit)


def row(vector):
    return vector[...].reshape(1, vector.shape[0])


def normalise(tokens):
    wide = tokens.astype(F32)
    row_mean = jnp.mean(wide, axis=1, keepdims=True)
    centered = wide - row_mean
    variance = jnp.mean(centered * centered, axis=1, keepdims=True)
    inv_std = lax.rsqrt(variance + 1e-06)
    return wide, centered * inv_std, inv_std


def project_kernel(head_size, *refs):
    sources, out, held, sems, packed = refs[:7], refs[7], refs[8:15], refs[15], refs[16]
    tokens, shift, scale, gate, cot, out_w, qkv_w = held
    width = tokens.shape[1]
    copies = [
        pltpu.make_async_copy(source, target, sems.at[i])
        for i, (source, target) in enumerate(zip(sources[:6], held[:6]))
    ]
    parts = [slice(part * width, (part + 1) * width) for part in range(3)]
    copies += [
        pltpu.make_async_copy(sources[6].at[:, at], qkv_w.at[:, at], sems.at[6 + part])
        for part, at in enumerate(parts)
    ]
    for copy in copies:
        copy.start()
    for copy in copies[:5]:
        copy.wait()
    _, normed, _ = normalise(tokens[...])
    modulated = (normed * (1.0 + row(scale)) + row(shift)).astype(BF16)
    gated = (row(gate) * cot[...].astype(F32)).astype(BF16)
    copies[5].wait()
    pulled = lax.dot_general(
        out_w[...], gated, (((1,), (1,)), ((), ())), preferred_element_type=F32
    )

    def part_of(part):
        copies[6 + part].wait()
        return jnp.dot(modulated, qkv_w[:, parts[part]], preferred_element_type=F32).T

    def send(first, second, half):
        rows = slice(half * 2 * head_size, (half + 1) * 2 * head_size)
        for head in range(H):
            at = slice(head * head_size, (head + 1) * head_size)
            packed[head, rows, :] = jnp.concatenate([first[at], second[at]], axis=0).astype(BF16)
        copy = pltpu.make_async_copy(packed.at[:, rows, :], out.at[:, rows, :], sems.at[9 + half])
        copy.start()
        return copy

    leaving = [send(part_of(0), part_of(1), 0)]
    leaving.append(send(part_of(2), pulled, 1))
    for copy in leaving:
        copy.wait()


def project(tokens, shift, scale, gate, qkv_w, out_w, cot):
    tok_rows, width = tokens.shape
    head_size = width // H
    operands = (tokens, shift, scale, gate, cot, out_w, qkv_w)
    hbm = pl.BlockSpec(memory_space=pl.ANY)
    packed = (H, 4 * head_size, tok_rows)
    return pl.pallas_call(
        functools.partial(project_kernel, head_size),
        in_specs=[hbm] * 7,
        out_specs=hbm,
        out_shape=jax.ShapeDtypeStruct(packed, BF16),
        scratch_shapes=[pltpu.VMEM(x.shape, x.dtype) for x in operands]
        + [pltpu.SemaphoreType.DMA((11,)), pltpu.VMEM(packed, BF16)],
        compiler_params=pltpu.CompilerParams(vmem_limit_bytes=PROJECT_LIMIT),
        name="project",
    )(*operands)


def attend_kernel(head_size, group, split, items, weight, *refs):
    if split:
        pairs, held, near, far = refs[:4]
        refs = refs[4:]
    else:
        held, near = refs[:2]
        refs = refs[2:]
    key_rows, value_rows, key_cols, value_cols, key_grad, value_grad, near_flat, sem = refs
    step = pl.program_id(0)
    load = pltpu.make_async_copy(weight, held, sem)
    chunks = items.shape[0]
    key_chunks = key_rows.shape[0] // LANES
    att_scale = 1.0 / math.sqrt(head_size)
    exponent_scale = att_scale * math.log2(math.e)
    pad = value_rows.shape[1] - head_size

    @pl.when(step == 0)
    def _():
        load.start()
        for s in range(key_chunks):
            if split:
                pair = pairs[s].astype(F32)
            else:
                pair = items[s].astype(F32)[head_size : 3 * head_size]
            at = slice(s * LANES, (s + 1) * LANES)
            keys, values = pair[:head_size], pair[head_size:]
            key_cols[:, at] = keys.astype(BF16)
            value_cols[:, at] = values.astype(BF16)
            key_rows[at, :] = keys.T.astype(BF16)
            value_rows[at, :] = jnp.concatenate(
                [values, jnp.ones((pad, LANES), F32)], axis=0
            ).T.astype(BF16)
        key_grad[...] = jnp.zeros_like(key_grad)
        value_grad[...] = jnp.zeros_like(value_grad)

    block = [items[step * group + g].astype(F32) for g in range(group)]
    queries = jnp.concatenate([b[:head_size] for b in block], axis=1)
    grads = jnp.concatenate([b[3 * head_size :] for b in block], axis=1)
    scores = jnp.dot(key_rows[...], queries.astype(BF16), preferred_element_type=F32)
    row_max = jnp.max(scores, axis=0, keepdims=True)
    exponent = jnp.exp2((scores - row_max) * exponent_scale)
    total = jnp.sum(exponent, axis=0, keepdims=True)
    weights = (exponent * (1.0 / total)).astype(BF16)
    attended = (
        jnp.dot(value_cols[...], weights, preferred_element_type=F32).astype(BF16).astype(F32)
    )
    less = -jnp.sum(attended * grads, axis=0, keepdims=True)
    less_high = less.astype(BF16).astype(F32)
    less_mid = (less - less_high).astype(BF16).astype(F32)
    less_low = less - less_high - less_mid
    place = lax.broadcasted_iota(jnp.int32, (pad, less.shape[1]), 0)
    tail = jnp.where(
        place == 0, less_high, jnp.where(place == 1, less_mid, jnp.where(place == 2, less_low, 0.0))
    )
    centred_grad = jnp.dot(
        value_rows[...],
        jnp.concatenate([grads, tail], axis=0).astype(BF16),
        preferred_element_type=F32,
    )
    score_grad = (weights.astype(F32) * centred_grad * att_scale).astype(BF16)
    query_grad = jnp.dot(key_cols[...], score_grad, preferred_element_type=F32)
    key_grad[...] += jnp.dot(score_grad, queries.T.astype(BF16), preferred_element_type=F32)
    value_grad[...] += jnp.dot(weights, grads.T.astype(BF16), preferred_element_type=F32)
    for g in range(group):
        at = slice(g * LANES, (g + 1) * LANES)
        near_flat[step * group + g] = jnp.concatenate(
            [attended[:, at], query_grad[:, at]], axis=0
        )

    @pl.when(step == pl.num_programs(0) - 1)
    def _():
        for s in range(key_chunks):
            at = slice(s * LANES, (s + 1) * LANES)
            grads_of = jnp.concatenate([key_grad[at, :].T, value_grad[at, :].T], axis=0)
            if split:
                far[s] = grads_of
            else:
                near[s] = jnp.concatenate([near_flat[s], grads_of], axis=0).astype(BF16)
        if split:
            near[...] = near_flat[...].astype(BF16)
        load.wait()


def attend(items, weight, pairs=None):
    chunks = items.shape[0]
    head_size = items.shape[1] // 4
    split = pairs is not None
    key_chunks = pairs.shape[0] if split else chunks
    key_len = key_chunks * LANES
    group = math.gcd(chunks, max(1, SCORE_LIMIT // (key_len * LANES)))
    pad = 8
    whole = lambda shape: pl.BlockSpec(shape, lambda i: (0,) * len(shape))
    if split:
        shapes = [
            jax.ShapeDtypeStruct((chunks, 2 * head_size, LANES), BF16),
            jax.ShapeDtypeStruct((key_chunks, 2 * head_size, LANES), F32),
        ]
        operands = (items, weight, pairs)
    else:
        shapes = [jax.ShapeDtypeStruct((chunks, 4 * head_size, LANES), BF16)]
        operands = (items, weight)
    specs = [whole(x.shape) for x in operands]
    specs[1] = pl.BlockSpec(memory_space=pl.ANY)
    shapes = [jax.ShapeDtypeStruct(weight.shape, weight.dtype)] + shapes
    return pl.pallas_call(
        functools.partial(attend_kernel, head_size, group, split),
        grid=(chunks // group,),
        in_specs=specs,
        out_specs=[pl.BlockSpec(memory_space=pltpu.VMEM)] + [whole(x.shape) for x in shapes[1:]],
        out_shape=shapes,
        scratch_shapes=[
            pltpu.VMEM((key_len, head_size), BF16),
            pltpu.VMEM((key_len, head_size + pad), BF16),
            pltpu.VMEM((head_size, key_len), BF16),
            pltpu.VMEM((head_size, key_len), BF16),
            pltpu.VMEM((key_len, head_size), F32),
            pltpu.VMEM((key_len, head_size), F32),
            pltpu.VMEM((chunks, 2 * head_size, LANES), F32),
            pltpu.SemaphoreType.DMA,
        ],
        compiler_params=params(ATTEND_LIMIT),
        name="attend",
    )(*operands)


def gather_kernel(
    head_size, items, tokens, qkv_w, out_w, cot, branch, mod_grad, sums, grad_cols
):
    width = tokens.shape[1]
    flat = [items[head].astype(F32) for head in range(H)]
    for part in range(3):
        grad_cols[part * width : (part + 1) * width, :] = jnp.concatenate(
            [x[(part + 1) * head_size : (part + 2) * head_size] for x in flat], axis=0
        ).astype(BF16)
    att = jnp.concatenate([x[:head_size] for x in flat], axis=0).T.astype(BF16)
    out = jnp.dot(att, out_w[...], preferred_element_type=F32)
    back = jnp.dot(qkv_w[...], grad_cols[...], preferred_element_type=F32).T
    _, normed, _ = normalise(tokens[...])
    branch[...] = out
    mod_grad[...] = back
    sums[...] = jnp.concatenate(
        [
            jnp.sum(back, axis=0, keepdims=True),
            jnp.sum(back * normed, axis=0, keepdims=True),
            jnp.sum(cot[...].astype(F32) * out, axis=0, keepdims=True),
        ],
        axis=0,
    )


def gather(items, tokens, qkv_w, out_w, cot):
    tok_rows, width = tokens.shape
    vmem = pl.BlockSpec(memory_space=pltpu.VMEM)
    return pl.pallas_call(
        functools.partial(gather_kernel, width // H),
        in_specs=[vmem] * 5,
        out_specs=[vmem] * 3,
        out_shape=[
            jax.ShapeDtypeStruct((tok_rows, width), F32),
            jax.ShapeDtypeStruct((tok_rows, width), F32),
            jax.ShapeDtypeStruct((3, width), F32),
        ],
        scratch_shapes=[pltpu.VMEM((3 * width, tok_rows), BF16)],
        compiler_params=pltpu.CompilerParams(vmem_limit_bytes=FINISH_LIMIT),
        name="gather",
    )(items, tokens, qkv_w, out_w, cot)


def finish_kernel(branch, mod_grad, tokens, scale, gate, cot, block_output, grad_input):
    wide, normed, inv_std = normalise(tokens[...])
    block_output[...] = (wide + row(gate) * branch[...]).astype(BF16)
    normed_grad = mod_grad[...] * (1.0 + row(scale))
    first_mean = jnp.mean(normed_grad, axis=1, keepdims=True)
    second_mean = jnp.mean(normed_grad * normed, axis=1, keepdims=True)
    grad_input[...] = (
        cot[...].astype(F32) + inv_std * (normed_grad - first_mean - normed * second_mean)
    ).astype(BF16)


def finish(branch, mod_grad, tokens, scale, gate, cot):
    vmem = pl.BlockSpec(memory_space=pltpu.VMEM)
    return pl.pallas_call(
        finish_kernel,
        in_specs=[vmem] * 6,
        out_specs=[vmem] * 2,
        out_shape=[jax.ShapeDtypeStruct(tokens.shape, BF16)] * 2,
        compiler_params=pltpu.CompilerParams(vmem_limit_bytes=FINISH_LIMIT),
        cost_estimate=pl.CostEstimate(
            flops=30 * tokens.size, transcendentals=0, bytes_accessed=16 * tokens.size
        ),
        name="finish",
    )(branch, mod_grad, tokens, scale, gate, cot)


def from_partner(shard, axis, stride):
    return lax.ppermute(shard, axis, [(i, i ^ stride) for i in range(lax.axis_size(axis))])


def exchange(blocks):
    return lax.all_to_all(blocks, "seq", split_axis=0, concat_axis=0, tiled=True)


def per_device(tokens, shift_cond, scale_cond, gate_cond, qkv_weight, out_weight, cotangent):
    seq_count = lax.axis_size("seq")
    repeat = seq_count // H
    levels = repeat.bit_length() - 1
    tok_rows, width = tokens.shape
    head_size = width // H
    sub_rows = tok_rows // repeat
    packed = project(tokens, shift_cond, scale_cond, gate_cond, qkv_weight, out_weight, cotangent)
    if repeat == 1:
        held, made = attend(exchange(packed), qkv_weight)
        returned = exchange(made)
    else:
        packed = packed.reshape(H, 4 * head_size, repeat, sub_rows).transpose(0, 2, 1, 3)
        landed = exchange(packed.reshape(seq_count, 4 * head_size, sub_rows))
        items = landed.reshape(H, repeat, 4 * head_size, sub_rows).transpose(0, 2, 1, 3)
        items = items.reshape(H, 4 * head_size, tok_rows)
        pairs = items[:, head_size : 3 * head_size]
        for level in range(levels):
            pairs = jnp.concatenate([pairs, from_partner(pairs, "seq", 1 << level)], axis=0)
        held, near, far = attend(items, qkv_weight, pairs)
        for level in reversed(range(levels)):
            middle = far.shape[0] // 2
            far = far[:middle] + from_partner(far[middle:], "seq", 1 << level)
        made = jnp.concatenate([near, far.astype(BF16)], axis=1)
        made = made.reshape(H, 4 * head_size, repeat, sub_rows).transpose(0, 2, 1, 3)
        back = exchange(made.reshape(seq_count, 4 * head_size, sub_rows))
        returned = back.reshape(H, repeat, 4 * head_size, sub_rows).transpose(0, 2, 1, 3)
        returned = returned.reshape(H, 4 * head_size, tok_rows)
    branch, mod_grad, sums = gather(returned, tokens, held, out_weight, cotangent)
    block_output, grad_input = finish(
        branch, mod_grad, tokens, scale_cond, gate_cond, cotangent
    )
    stride = 1
    while stride < seq_count:
        if 4 * stride <= seq_count:
            first, second, third = (from_partner(sums, "seq", k * stride) for k in (1, 2, 3))
            sums = (sums + first) + (second + third)
            stride *= 4
        else:
            sums = sums + from_partner(sums, "seq", stride)
            stride *= 2
    return (block_output, grad_input, sums / math.sqrt(tok_rows * seq_count))


def solution(mesh):
    return jax.shard_map(
        per_device,
        mesh=mesh,
        in_specs=(
            P(("groups", "seq"), None),
            P("groups"),
            P("groups"),
            P("groups"),
            P(),
            P(),
            P(("groups", "seq"), None),
        ),
        out_specs=(P(("groups", "seq"), None), P(("groups", "seq"), None), P("groups", None)),
        check_vma=False,
    )
```

```python
import functools
import math

import jax
import jax.numpy as jnp
from jax import lax
from jax.experimental import pallas as pl
from jax.experimental.pallas import tpu as pltpu
from jax.sharding import PartitionSpec as P

H = 16
LANES = 128
SCORE_LIMIT = 2048 * 2048
F32 = jnp.float32
BF16 = jnp.bfloat16
PROJECT_LIMIT = 60 * 1024 * 1024
ATTEND_LIMIT = 44 * 1024 * 1024
FINISH_LIMIT = 24 * 1024 * 1024


def params(limit):
    return pltpu.CompilerParams(dimension_semantics=("arbitrary",), vmem_limit_bytes=limit)


def row(vector):
    return vector[...].reshape(1, vector.shape[0])


def normalise(tokens):
    wide = tokens.astype(F32)
    row_mean = jnp.mean(wide, axis=1, keepdims=True)
    centered = wide - row_mean
    variance = jnp.mean(centered * centered, axis=1, keepdims=True)
    inv_std = lax.rsqrt(variance + 1e-06)
    return wide, centered * inv_std, inv_std


def project_kernel(head_size, *refs):
    sources, out, held, sems, packed = refs[:7], refs[7], refs[8:15], refs[15], refs[16]
    tokens, shift, scale, gate, cot, out_w, qkv_w = held
    width = tokens.shape[1]
    copies = [
        pltpu.make_async_copy(source, target, sems.at[i])
        for i, (source, target) in enumerate(zip(sources[:6], held[:6]))
    ]
    parts = [slice(part * width, (part + 1) * width) for part in range(3)]
    copies += [
        pltpu.make_async_copy(sources[6].at[:, at], qkv_w.at[:, at], sems.at[6 + part])
        for part, at in enumerate(parts)
    ]
    for copy in copies:
        copy.start()
    for copy in copies[:5]:
        copy.wait()
    _, normed, _ = normalise(tokens[...])
    modulated = (normed * (1.0 + row(scale)) + row(shift)).astype(BF16)
    gated = (row(gate) * cot[...].astype(F32)).astype(BF16)
    copies[5].wait()
    pulled = lax.dot_general(
        out_w[...], gated, (((1,), (1,)), ((), ())), preferred_element_type=F32
    )

    def part_of(part):
        copies[6 + part].wait()
        return jnp.dot(modulated, qkv_w[:, parts[part]], preferred_element_type=F32).T

    def send(first, second, half):
        rows = slice(half * 2 * head_size, (half + 1) * 2 * head_size)
        for head in range(H):
            at = slice(head * head_size, (head + 1) * head_size)
            packed[head, rows, :] = jnp.concatenate([first[at], second[at]], axis=0).astype(BF16)
        copy = pltpu.make_async_copy(packed.at[:, rows, :], out.at[:, rows, :], sems.at[9 + half])
        copy.start()
        return copy

    leaving = [send(part_of(0), part_of(1), 0)]
    leaving.append(send(part_of(2), pulled, 1))
    for copy in leaving:
        copy.wait()


def project(tokens, shift, scale, gate, qkv_w, out_w, cot):
    tok_rows, width = tokens.shape
    head_size = width // H
    operands = (tokens, shift, scale, gate, cot, out_w, qkv_w)
    hbm = pl.BlockSpec(memory_space=pl.ANY)
    packed = (H, 4 * head_size, tok_rows)
    return pl.pallas_call(
        functools.partial(project_kernel, head_size),
        in_specs=[hbm] * 7,
        out_specs=hbm,
        out_shape=jax.ShapeDtypeStruct(packed, BF16),
        scratch_shapes=[pltpu.VMEM(x.shape, x.dtype) for x in operands]
        + [pltpu.SemaphoreType.DMA((11,)), pltpu.VMEM(packed, BF16)],
        compiler_params=pltpu.CompilerParams(vmem_limit_bytes=PROJECT_LIMIT),
        name="project",
    )(*operands)


def attend_kernel(head_size, group, split, items, weight, *refs):
    if split:
        pairs, held, near, far = refs[:4]
        refs = refs[4:]
    else:
        held, near = refs[:2]
        refs = refs[2:]
    key_rows, value_rows, key_cols, value_cols, key_grad, value_grad, near_flat, sem = refs
    step = pl.program_id(0)
    single = not split and group == items.shape[0]
    load = pltpu.make_async_copy(weight, held, sem)
    chunks = items.shape[0]
    key_chunks = key_rows.shape[0] // LANES
    att_scale = 1.0 / math.sqrt(head_size)
    exponent_scale = att_scale * math.log2(math.e)
    pad = value_rows.shape[1] - head_size

    @pl.when(step == 0)
    def _():
        load.start()
        for s in range(key_chunks):
            if split:
                pair = pairs[s].astype(F32)
            else:
                pair = items[s].astype(F32)[head_size : 3 * head_size]
            at = slice(s * LANES, (s + 1) * LANES)
            keys, values = pair[:head_size], pair[head_size:]
            key_cols[:, at] = keys.astype(BF16)
            value_cols[:, at] = values.astype(BF16)
            key_rows[at, :] = keys.T.astype(BF16)
            value_rows[at, :] = jnp.concatenate(
                [values, jnp.ones((pad, LANES), F32)], axis=0
            ).T.astype(BF16)
        if not single:
            key_grad[...] = jnp.zeros_like(key_grad)
            value_grad[...] = jnp.zeros_like(value_grad)

    block = [items[step * group + g].astype(F32) for g in range(group)]
    queries = jnp.concatenate([b[:head_size] for b in block], axis=1)
    grads = jnp.concatenate([b[3 * head_size :] for b in block], axis=1)
    scores = jnp.dot(key_rows[...], queries.astype(BF16), preferred_element_type=F32)
    row_max = jnp.max(scores, axis=0, keepdims=True)
    exponent = jnp.exp2((scores - row_max) * exponent_scale)
    total = jnp.sum(exponent, axis=0, keepdims=True)
    weights = (exponent * (1.0 / total)).astype(BF16)
    attended = (
        jnp.dot(value_cols[...], weights, preferred_element_type=F32).astype(BF16).astype(F32)
    )
    less = -jnp.sum(attended * grads, axis=0, keepdims=True)
    less_high = less.astype(BF16).astype(F32)
    less_mid = (less - less_high).astype(BF16).astype(F32)
    less_low = less - less_high - less_mid
    place = lax.broadcasted_iota(jnp.int32, (pad, less.shape[1]), 0)
    tail = jnp.where(
        place == 0, less_high, jnp.where(place == 1, less_mid, jnp.where(place == 2, less_low, 0.0))
    )
    centred_grad = jnp.dot(
        value_rows[...],
        jnp.concatenate([grads, tail], axis=0).astype(BF16),
        preferred_element_type=F32,
    )
    score_grad = (weights.astype(F32) * centred_grad * att_scale).astype(BF16)
    query_grad = jnp.dot(key_cols[...], score_grad, preferred_element_type=F32)
    keys_of = jnp.dot(score_grad, queries.T.astype(BF16), preferred_element_type=F32)
    values_of = jnp.dot(weights, grads.T.astype(BF16), preferred_element_type=F32)
    if single:
        for s in range(key_chunks):
            at = slice(s * LANES, (s + 1) * LANES)
            near[s] = jnp.concatenate(
                [attended[:, at], query_grad[:, at], keys_of[at, :].T, values_of[at, :].T], axis=0
            ).astype(BF16)
        load.wait()
        return
    key_grad[...] += keys_of
    value_grad[...] += values_of
    for g in range(group):
        at = slice(g * LANES, (g + 1) * LANES)
        near_flat[step * group + g] = jnp.concatenate(
            [attended[:, at], query_grad[:, at]], axis=0
        )

    @pl.when(step == pl.num_programs(0) - 1)
    def _():
        for s in range(key_chunks):
            at = slice(s * LANES, (s + 1) * LANES)
            grads_of = jnp.concatenate([key_grad[at, :].T, value_grad[at, :].T], axis=0)
            if split:
                far[s] = grads_of
            else:
                near[s] = jnp.concatenate([near_flat[s], grads_of], axis=0).astype(BF16)
        if split:
            near[...] = near_flat[...].astype(BF16)
        load.wait()


def attend(items, weight, pairs=None):
    chunks = items.shape[0]
    head_size = items.shape[1] // 4
    split = pairs is not None
    key_chunks = pairs.shape[0] if split else chunks
    key_len = key_chunks * LANES
    group = math.gcd(chunks, max(1, SCORE_LIMIT // (key_len * LANES)))
    pad = 8
    whole = lambda shape: pl.BlockSpec(shape, lambda i: (0,) * len(shape))
    if split:
        shapes = [
            jax.ShapeDtypeStruct((chunks, 2 * head_size, LANES), BF16),
            jax.ShapeDtypeStruct((key_chunks, 2 * head_size, LANES), F32),
        ]
        operands = (items, weight, pairs)
    else:
        shapes = [jax.ShapeDtypeStruct((chunks, 4 * head_size, LANES), BF16)]
        operands = (items, weight)
    specs = [whole(x.shape) for x in operands]
    specs[1] = pl.BlockSpec(memory_space=pl.ANY)
    shapes = [jax.ShapeDtypeStruct(weight.shape, weight.dtype)] + shapes
    return pl.pallas_call(
        functools.partial(attend_kernel, head_size, group, split),
        grid=(chunks // group,),
        in_specs=specs,
        out_specs=[pl.BlockSpec(memory_space=pltpu.VMEM)] + [whole(x.shape) for x in shapes[1:]],
        out_shape=shapes,
        scratch_shapes=[
            pltpu.VMEM((key_len, head_size), BF16),
            pltpu.VMEM((key_len, head_size + pad), BF16),
            pltpu.VMEM((head_size, key_len), BF16),
            pltpu.VMEM((head_size, key_len), BF16),
            pltpu.VMEM((key_len, head_size), F32),
            pltpu.VMEM((key_len, head_size), F32),
            pltpu.VMEM((chunks, 2 * head_size, LANES), F32),
            pltpu.SemaphoreType.DMA,
        ],
        compiler_params=params(ATTEND_LIMIT),
        name="attend",
    )(*operands)


def gather_kernel(
    head_size, items, tokens, qkv_w, out_w, cot, branch, mod_grad, sums, grad_cols
):
    width = tokens.shape[1]
    flat = [items[head].astype(F32) for head in range(H)]
    back = jnp.zeros((width, tokens.shape[0]), F32)
    for part in range(3):
        at = slice(part * width, (part + 1) * width)
        grad_cols[at, :] = jnp.concatenate(
            [x[(part + 1) * head_size : (part + 2) * head_size] for x in flat], axis=0
        ).astype(BF16)
        back = back + jnp.dot(qkv_w[:, at], grad_cols[at, :], preferred_element_type=F32)
    back = back.T
    att = jnp.concatenate([x[:head_size] for x in flat], axis=0).T.astype(BF16)
    out = jnp.dot(att, out_w[...], preferred_element_type=F32)
    _, normed, _ = normalise(tokens[...])
    branch[...] = out
    mod_grad[...] = back
    sums[...] = jnp.concatenate(
        [
            jnp.sum(back, axis=0, keepdims=True),
            jnp.sum(back * normed, axis=0, keepdims=True),
            jnp.sum(cot[...].astype(F32) * out, axis=0, keepdims=True),
        ],
        axis=0,
    )


def gather(items, tokens, qkv_w, out_w, cot):
    tok_rows, width = tokens.shape
    vmem = pl.BlockSpec(memory_space=pltpu.VMEM)
    return pl.pallas_call(
        functools.partial(gather_kernel, width // H),
        in_specs=[vmem] * 5,
        out_specs=[vmem] * 3,
        out_shape=[
            jax.ShapeDtypeStruct((tok_rows, width), F32),
            jax.ShapeDtypeStruct((tok_rows, width), F32),
            jax.ShapeDtypeStruct((3, width), F32),
        ],
        scratch_shapes=[pltpu.VMEM((3 * width, tok_rows), BF16)],
        compiler_params=pltpu.CompilerParams(vmem_limit_bytes=FINISH_LIMIT),
        name="gather",
    )(items, tokens, qkv_w, out_w, cot)


def finish_kernel(branch, mod_grad, tokens, scale, gate, cot, block_output, grad_input):
    wide, normed, inv_std = normalise(tokens[...])
    block_output[...] = (wide + row(gate) * branch[...]).astype(BF16)
    normed_grad = mod_grad[...] * (1.0 + row(scale))
    first_mean = jnp.mean(normed_grad, axis=1, keepdims=True)
    second_mean = jnp.mean(normed_grad * normed, axis=1, keepdims=True)
    grad_input[...] = (
        cot[...].astype(F32) + inv_std * (normed_grad - first_mean - normed * second_mean)
    ).astype(BF16)


def finish(branch, mod_grad, tokens, scale, gate, cot):
    vmem = pl.BlockSpec(memory_space=pltpu.VMEM)
    return pl.pallas_call(
        finish_kernel,
        in_specs=[vmem] * 6,
        out_specs=[vmem] * 2,
        out_shape=[jax.ShapeDtypeStruct(tokens.shape, BF16)] * 2,
        compiler_params=pltpu.CompilerParams(vmem_limit_bytes=FINISH_LIMIT),
        cost_estimate=pl.CostEstimate(
            flops=30 * tokens.size, transcendentals=0, bytes_accessed=16 * tokens.size
        ),
        name="finish",
    )(branch, mod_grad, tokens, scale, gate, cot)


def from_partner(shard, axis, stride):
    return lax.ppermute(shard, axis, [(i, i ^ stride) for i in range(lax.axis_size(axis))])


def exchange(blocks):
    return lax.all_to_all(blocks, "seq", split_axis=0, concat_axis=0, tiled=True)


def per_device(tokens, shift_cond, scale_cond, gate_cond, qkv_weight, out_weight, cotangent):
    seq_count = lax.axis_size("seq")
    repeat = seq_count // H
    levels = repeat.bit_length() - 1
    tok_rows, width = tokens.shape
    head_size = width // H
    sub_rows = tok_rows // repeat
    packed = project(tokens, shift_cond, scale_cond, gate_cond, qkv_weight, out_weight, cotangent)
    if repeat == 1:
        held, made = attend(exchange(packed), qkv_weight)
        returned = exchange(made)
    else:
        packed = packed.reshape(H, 4 * head_size, repeat, sub_rows).transpose(0, 2, 1, 3)
        landed = exchange(packed.reshape(seq_count, 4 * head_size, sub_rows))
        items = landed.reshape(H, repeat, 4 * head_size, sub_rows).transpose(0, 2, 1, 3)
        items = items.reshape(H, 4 * head_size, tok_rows)
        pairs = items[:, head_size : 3 * head_size]
        for level in range(levels):
            pairs = jnp.concatenate([pairs, from_partner(pairs, "seq", 1 << level)], axis=0)
        held, near, far = attend(items, qkv_weight, pairs)
        for level in reversed(range(levels)):
            middle = far.shape[0] // 2
            far = far[:middle] + from_partner(far[middle:], "seq", 1 << level)
        made = jnp.concatenate([near, far.astype(BF16)], axis=1)
        made = made.reshape(H, 4 * head_size, repeat, sub_rows).transpose(0, 2, 1, 3)
        back = exchange(made.reshape(seq_count, 4 * head_size, sub_rows))
        returned = back.reshape(H, repeat, 4 * head_size, sub_rows).transpose(0, 2, 1, 3)
        returned = returned.reshape(H, 4 * head_size, tok_rows)
    branch, mod_grad, sums = gather(returned, tokens, held, out_weight, cotangent)
    block_output, grad_input = finish(
        branch, mod_grad, tokens, scale_cond, gate_cond, cotangent
    )
    stride = 1
    while stride < seq_count:
        if 4 * stride <= seq_count:
            first, second, third = (from_partner(sums, "seq", k * stride) for k in (1, 2, 3))
            sums = (sums + first) + (second + third)
            stride *= 4
        else:
            sums = sums + from_partner(sums, "seq", stride)
            stride *= 2
    return (block_output, grad_input, sums / math.sqrt(tok_rows * seq_count))


def solution(mesh):
    return jax.shard_map(
        per_device,
        mesh=mesh,
        in_specs=(
            P(("groups", "seq"), None),
            P("groups"),
            P("groups"),
            P("groups"),
            P(),
            P(),
            P(("groups", "seq"), None),
        ),
        out_specs=(P(("groups", "seq"), None), P(("groups", "seq"), None), P("groups", None)),
        check_vma=False,
    )
```

```python
import functools
import math

import jax
import jax.numpy as jnp
from jax import lax
from jax.experimental import pallas as pl
from jax.experimental.pallas import tpu as pltpu
from jax.sharding import PartitionSpec as P

H = 16
LANES = 128
SCORE_LIMIT = 2048 * 2048
F32 = jnp.float32
BF16 = jnp.bfloat16
PROJECT_LIMIT = 60 * 1024 * 1024
ATTEND_LIMIT = 44 * 1024 * 1024
FINISH_LIMIT = 24 * 1024 * 1024


def params(limit):
    return pltpu.CompilerParams(dimension_semantics=("arbitrary",), vmem_limit_bytes=limit)


def row(vector):
    return vector[...].reshape(1, vector.shape[0])


def normalise(tokens):
    wide = tokens.astype(F32)
    row_mean = jnp.mean(wide, axis=1, keepdims=True)
    centered = wide - row_mean
    variance = jnp.mean(centered * centered, axis=1, keepdims=True)
    inv_std = lax.rsqrt(variance + 1e-06)
    return wide, centered * inv_std, inv_std


def project_kernel(head_size, *refs):
    sources, out, held, sems, packed = refs[:7], refs[7], refs[8:15], refs[15], refs[16]
    tokens, shift, scale, gate, cot, out_w, qkv_w = held
    width = tokens.shape[1]
    copies = [
        pltpu.make_async_copy(source, target, sems.at[i])
        for i, (source, target) in enumerate(zip(sources[:6], held[:6]))
    ]
    parts = [slice(part * width, (part + 1) * width) for part in range(3)]
    copies += [
        pltpu.make_async_copy(sources[6].at[:, at], qkv_w.at[:, at], sems.at[6 + part])
        for part, at in enumerate(parts)
    ]
    for copy in copies[:5] + copies[6:] + copies[5:6]:
        copy.start()
    for copy in copies[:3]:
        copy.wait()
    _, normed, _ = normalise(tokens[...])
    modulated = (normed * (1.0 + row(scale)) + row(shift)).astype(BF16)

    def pulled_of():
        copies[3].wait()
        copies[4].wait()
        gated = (row(gate) * cot[...].astype(F32)).astype(BF16)
        copies[5].wait()
        return lax.dot_general(
            out_w[...], gated, (((1,), (1,)), ((), ())), preferred_element_type=F32
        )

    def part_of(part):
        copies[6 + part].wait()
        return jnp.dot(modulated, qkv_w[:, parts[part]], preferred_element_type=F32).T

    def send(first, second, half):
        rows = slice(half * 2 * head_size, (half + 1) * 2 * head_size)
        for head in range(H):
            at = slice(head * head_size, (head + 1) * head_size)
            packed[head, rows, :] = jnp.concatenate([first[at], second[at]], axis=0).astype(BF16)
        copy = pltpu.make_async_copy(packed.at[:, rows, :], out.at[:, rows, :], sems.at[9 + half])
        copy.start()
        return copy

    leaving = [send(part_of(0), part_of(1), 0)]
    leaving.append(send(part_of(2), pulled_of(), 1))
    for copy in leaving:
        copy.wait()


def project(tokens, shift, scale, gate, qkv_w, out_w, cot):
    tok_rows, width = tokens.shape
    head_size = width // H
    operands = (tokens, shift, scale, gate, cot, out_w, qkv_w)
    hbm = pl.BlockSpec(memory_space=pl.ANY)
    packed = (H, 4 * head_size, tok_rows)
    return pl.pallas_call(
        functools.partial(project_kernel, head_size),
        in_specs=[hbm] * 7,
        out_specs=hbm,
        out_shape=jax.ShapeDtypeStruct(packed, BF16),
        scratch_shapes=[pltpu.VMEM(x.shape, x.dtype) for x in operands]
        + [pltpu.SemaphoreType.DMA((11,)), pltpu.VMEM(packed, BF16)],
        compiler_params=pltpu.CompilerParams(vmem_limit_bytes=PROJECT_LIMIT),
        name="project",
    )(*operands)


def attend_kernel(head_size, group, split, items, weight, *refs):
    if split:
        pairs, held, near, far = refs[:4]
        refs = refs[4:]
    else:
        held, near = refs[:2]
        refs = refs[2:]
    key_rows, value_rows, key_cols, value_cols, key_grad, value_grad, near_flat, sem = refs
    step = pl.program_id(0)
    single = not split and group == items.shape[0]
    load = pltpu.make_async_copy(weight, held, sem)
    chunks = items.shape[0]
    key_chunks = key_rows.shape[0] // LANES
    att_scale = 1.0 / math.sqrt(head_size)
    exponent_scale = att_scale * math.log2(math.e)
    pad = value_rows.shape[1] - head_size

    @pl.when(step == 0)
    def _():
        load.start()
        for s in range(key_chunks):
            if split:
                pair = pairs[s].astype(F32)
            else:
                pair = items[s].astype(F32)[head_size : 3 * head_size]
            at = slice(s * LANES, (s + 1) * LANES)
            keys, values = pair[:head_size], pair[head_size:]
            key_cols[:, at] = keys.astype(BF16)
            value_cols[:, at] = values.astype(BF16)
            key_rows[at, :] = keys.T.astype(BF16)
            value_rows[at, :] = jnp.concatenate(
                [values, jnp.ones((pad, LANES), F32)], axis=0
            ).T.astype(BF16)
        if not single:
            key_grad[...] = jnp.zeros_like(key_grad)
            value_grad[...] = jnp.zeros_like(value_grad)

    block = [items[step * group + g].astype(F32) for g in range(group)]
    queries = jnp.concatenate([b[:head_size] for b in block], axis=1)
    grads = jnp.concatenate([b[3 * head_size :] for b in block], axis=1)
    scores = jnp.dot(key_rows[...], queries.astype(BF16), preferred_element_type=F32)
    row_max = jnp.max(scores, axis=0, keepdims=True)
    exponent = jnp.exp2((scores - row_max) * exponent_scale)
    total = jnp.sum(exponent, axis=0, keepdims=True)
    weights = (exponent * (1.0 / total)).astype(BF16)
    attended = (
        jnp.dot(value_cols[...], weights, preferred_element_type=F32).astype(BF16).astype(F32)
    )
    less = -jnp.sum(attended * grads, axis=0, keepdims=True)
    less_high = less.astype(BF16).astype(F32)
    less_mid = (less - less_high).astype(BF16).astype(F32)
    less_low = less - less_high - less_mid
    place = lax.broadcasted_iota(jnp.int32, (pad, less.shape[1]), 0)
    tail = jnp.where(
        place == 0, less_high, jnp.where(place == 1, less_mid, jnp.where(place == 2, less_low, 0.0))
    )
    centred_grad = jnp.dot(
        value_rows[...],
        jnp.concatenate([grads, tail], axis=0).astype(BF16),
        preferred_element_type=F32,
    )
    score_grad = (weights.astype(F32) * centred_grad * att_scale).astype(BF16)
    query_grad = jnp.dot(key_cols[...], score_grad, preferred_element_type=F32)
    keys_of = jnp.dot(score_grad, queries.T.astype(BF16), preferred_element_type=F32)
    values_of = jnp.dot(weights, grads.T.astype(BF16), preferred_element_type=F32)
    if single:
        for s in range(key_chunks):
            at = slice(s * LANES, (s + 1) * LANES)
            near[s] = jnp.concatenate(
                [attended[:, at], query_grad[:, at], keys_of[at, :].T, values_of[at, :].T], axis=0
            ).astype(BF16)
        load.wait()
        return
    key_grad[...] += keys_of
    value_grad[...] += values_of
    for g in range(group):
        at = slice(g * LANES, (g + 1) * LANES)
        near_flat[step * group + g] = jnp.concatenate(
            [attended[:, at], query_grad[:, at]], axis=0
        )

    @pl.when(step == pl.num_programs(0) - 1)
    def _():
        for s in range(key_chunks):
            at = slice(s * LANES, (s + 1) * LANES)
            grads_of = jnp.concatenate([key_grad[at, :].T, value_grad[at, :].T], axis=0)
            if split:
                far[s] = grads_of
            else:
                near[s] = jnp.concatenate([near_flat[s], grads_of], axis=0).astype(BF16)
        if split:
            near[...] = near_flat[...].astype(BF16)
        load.wait()


def attend(items, weight, pairs=None):
    chunks = items.shape[0]
    head_size = items.shape[1] // 4
    split = pairs is not None
    key_chunks = pairs.shape[0] if split else chunks
    key_len = key_chunks * LANES
    group = math.gcd(chunks, max(1, SCORE_LIMIT // (key_len * LANES)))
    pad = 8
    whole = lambda shape: pl.BlockSpec(shape, lambda i: (0,) * len(shape))
    if split:
        shapes = [
            jax.ShapeDtypeStruct((chunks, 2 * head_size, LANES), BF16),
            jax.ShapeDtypeStruct((key_chunks, 2 * head_size, LANES), F32),
        ]
        operands = (items, weight, pairs)
    else:
        shapes = [jax.ShapeDtypeStruct((chunks, 4 * head_size, LANES), BF16)]
        operands = (items, weight)
    specs = [whole(x.shape) for x in operands]
    specs[1] = pl.BlockSpec(memory_space=pl.ANY)
    shapes = [jax.ShapeDtypeStruct(weight.shape, weight.dtype)] + shapes
    return pl.pallas_call(
        functools.partial(attend_kernel, head_size, group, split),
        grid=(chunks // group,),
        in_specs=specs,
        out_specs=[pl.BlockSpec(memory_space=pltpu.VMEM)] + [whole(x.shape) for x in shapes[1:]],
        out_shape=shapes,
        scratch_shapes=[
            pltpu.VMEM((key_len, head_size), BF16),
            pltpu.VMEM((key_len, head_size + pad), BF16),
            pltpu.VMEM((head_size, key_len), BF16),
            pltpu.VMEM((head_size, key_len), BF16),
            pltpu.VMEM((key_len, head_size), F32),
            pltpu.VMEM((key_len, head_size), F32),
            pltpu.VMEM((chunks, 2 * head_size, LANES), F32),
            pltpu.SemaphoreType.DMA,
        ],
        compiler_params=params(ATTEND_LIMIT),
        name="attend",
    )(*operands)


def gather_kernel(
    head_size, items, tokens, qkv_w, out_w, cot, branch, mod_grad, sums, grad_cols
):
    width = tokens.shape[1]
    flat = [items[head].astype(F32) for head in range(H)]
    back = jnp.zeros((width, tokens.shape[0]), F32)
    for part in range(3):
        at = slice(part * width, (part + 1) * width)
        grad_cols[at, :] = jnp.concatenate(
            [x[(part + 1) * head_size : (part + 2) * head_size] for x in flat], axis=0
        ).astype(BF16)
        back = back + jnp.dot(qkv_w[:, at], grad_cols[at, :], preferred_element_type=F32)
    back = back.T
    att = jnp.concatenate([x[:head_size] for x in flat], axis=0).T.astype(BF16)
    out = jnp.dot(att, out_w[...], preferred_element_type=F32)
    _, normed, _ = normalise(tokens[...])
    branch[...] = out
    mod_grad[...] = back
    sums[...] = jnp.concatenate(
        [
            jnp.sum(back, axis=0, keepdims=True),
            jnp.sum(back * normed, axis=0, keepdims=True),
            jnp.sum(cot[...].astype(F32) * out, axis=0, keepdims=True),
        ],
        axis=0,
    )


def gather(items, tokens, qkv_w, out_w, cot):
    tok_rows, width = tokens.shape
    vmem = pl.BlockSpec(memory_space=pltpu.VMEM)
    return pl.pallas_call(
        functools.partial(gather_kernel, width // H),
        in_specs=[vmem] * 5,
        out_specs=[vmem] * 3,
        out_shape=[
            jax.ShapeDtypeStruct((tok_rows, width), F32),
            jax.ShapeDtypeStruct((tok_rows, width), F32),
            jax.ShapeDtypeStruct((3, width), F32),
        ],
        scratch_shapes=[pltpu.VMEM((3 * width, tok_rows), BF16)],
        compiler_params=pltpu.CompilerParams(vmem_limit_bytes=FINISH_LIMIT),
        name="gather",
    )(items, tokens, qkv_w, out_w, cot)


def finish_kernel(branch, mod_grad, tokens, scale, gate, cot, block_output, grad_input):
    wide, normed, inv_std = normalise(tokens[...])
    block_output[...] = (wide + row(gate) * branch[...]).astype(BF16)
    normed_grad = mod_grad[...] * (1.0 + row(scale))
    first_mean = jnp.mean(normed_grad, axis=1, keepdims=True)
    second_mean = jnp.mean(normed_grad * normed, axis=1, keepdims=True)
    grad_input[...] = (
        cot[...].astype(F32) + inv_std * (normed_grad - first_mean - normed * second_mean)
    ).astype(BF16)


def finish(branch, mod_grad, tokens, scale, gate, cot):
    vmem = pl.BlockSpec(memory_space=pltpu.VMEM)
    return pl.pallas_call(
        finish_kernel,
        in_specs=[vmem] * 6,
        out_specs=[vmem] * 2,
        out_shape=[jax.ShapeDtypeStruct(tokens.shape, BF16)] * 2,
        compiler_params=pltpu.CompilerParams(vmem_limit_bytes=FINISH_LIMIT),
        cost_estimate=pl.CostEstimate(
            flops=30 * tokens.size, transcendentals=0, bytes_accessed=16 * tokens.size
        ),
        name="finish",
    )(branch, mod_grad, tokens, scale, gate, cot)


def from_partner(shard, axis, stride):
    return lax.ppermute(shard, axis, [(i, i ^ stride) for i in range(lax.axis_size(axis))])


def exchange(blocks):
    return lax.all_to_all(blocks, "seq", split_axis=0, concat_axis=0, tiled=True)


def per_device(tokens, shift_cond, scale_cond, gate_cond, qkv_weight, out_weight, cotangent):
    seq_count = lax.axis_size("seq")
    repeat = seq_count // H
    levels = repeat.bit_length() - 1
    tok_rows, width = tokens.shape
    head_size = width // H
    sub_rows = tok_rows // repeat
    packed = project(tokens, shift_cond, scale_cond, gate_cond, qkv_weight, out_weight, cotangent)
    if repeat == 1:
        held, made = attend(exchange(packed), qkv_weight)
        returned = exchange(made)
    else:
        packed = packed.reshape(H, 4 * head_size, repeat, sub_rows).transpose(0, 2, 1, 3)
        landed = exchange(packed.reshape(seq_count, 4 * head_size, sub_rows))
        items = landed.reshape(H, repeat, 4 * head_size, sub_rows).transpose(0, 2, 1, 3)
        items = items.reshape(H, 4 * head_size, tok_rows)
        pairs = items[:, head_size : 3 * head_size]
        for level in range(levels):
            pairs = jnp.concatenate([pairs, from_partner(pairs, "seq", 1 << level)], axis=0)
        held, near, far = attend(items, qkv_weight, pairs)
        for level in reversed(range(levels)):
            middle = far.shape[0] // 2
            far = far[:middle] + from_partner(far[middle:], "seq", 1 << level)
        made = jnp.concatenate([near, far.astype(BF16)], axis=1)
        made = made.reshape(H, 4 * head_size, repeat, sub_rows).transpose(0, 2, 1, 3)
        back = exchange(made.reshape(seq_count, 4 * head_size, sub_rows))
        returned = back.reshape(H, repeat, 4 * head_size, sub_rows).transpose(0, 2, 1, 3)
        returned = returned.reshape(H, 4 * head_size, tok_rows)
    branch, mod_grad, sums = gather(returned, tokens, held, out_weight, cotangent)
    block_output, grad_input = finish(
        branch, mod_grad, tokens, scale_cond, gate_cond, cotangent
    )
    stride = 1
    while stride < seq_count:
        if 4 * stride <= seq_count:
            first, second, third = (from_partner(sums, "seq", k * stride) for k in (1, 2, 3))
            sums = (sums + first) + (second + third)
            stride *= 4
        else:
            sums = sums + from_partner(sums, "seq", stride)
            stride *= 2
    return (block_output, grad_input, sums / math.sqrt(tok_rows * seq_count))


def solution(mesh):
    return jax.shard_map(
        per_device,
        mesh=mesh,
        in_specs=(
            P(("groups", "seq"), None),
            P("groups"),
            P("groups"),
            P("groups"),
            P(),
            P(),
            P(("groups", "seq"), None),
        ),
        out_specs=(P(("groups", "seq"), None), P(("groups", "seq"), None), P("groups", None)),
        check_vma=False,
    )
```

```python
import functools
import math

import jax
import jax.numpy as jnp
from jax import lax
from jax.experimental import pallas as pl
from jax.experimental.pallas import tpu as pltpu
from jax.sharding import PartitionSpec as P

H = 16
LANES = 128
SCORE_LIMIT = 2048 * 2048
F32 = jnp.float32
BF16 = jnp.bfloat16
PROJECT_LIMIT = 60 * 1024 * 1024
ATTEND_LIMIT = 44 * 1024 * 1024
FINISH_LIMIT = 24 * 1024 * 1024


def params(limit):
    return pltpu.CompilerParams(dimension_semantics=("arbitrary",), vmem_limit_bytes=limit)


def row(vector):
    return vector[...].reshape(1, vector.shape[0])


def normalise(tokens):
    wide = tokens.astype(F32)
    row_mean = jnp.mean(wide, axis=1, keepdims=True)
    centered = wide - row_mean
    variance = jnp.mean(centered * centered, axis=1, keepdims=True)
    inv_std = lax.rsqrt(variance + 1e-06)
    return wide, centered * inv_std, inv_std


def project_kernel(head_size, *refs):
    sources, out, held, sems, packed = refs[:7], refs[7], refs[8:15], refs[15], refs[16]
    tokens, shift, scale, gate, cot, out_w, qkv_w = held
    width = tokens.shape[1]
    copies = [
        pltpu.make_async_copy(source, target, sems.at[i])
        for i, (source, target) in enumerate(zip(sources[:6], held[:6]))
    ]
    parts = [slice(part * width, (part + 1) * width) for part in range(3)]
    copies += [
        pltpu.make_async_copy(sources[6].at[:, at], qkv_w.at[:, at], sems.at[6 + part])
        for part, at in enumerate(parts)
    ]
    middle = H // 2 * head_size
    halves = [slice(0, middle), slice(middle, width)]
    out_copies = [
        pltpu.make_async_copy(sources[5].at[at, :], out_w.at[at, :], sems.at[sem])
        for at, sem in zip(halves, (5, 11))
    ]
    for copy in copies[:5] + copies[6:] + out_copies:
        copy.start()
    for copy in copies[:3]:
        copy.wait()
    _, normed, _ = normalise(tokens[...])
    modulated = (normed * (1.0 + row(scale)) + row(shift)).astype(BF16)

    def pulled_of(i, gated):
        out_copies[i].wait()
        return lax.dot_general(
            out_w[halves[i], :], gated, (((1,), (1,)), ((), ())), preferred_element_type=F32
        )

    def part_of(part):
        copies[6 + part].wait()
        return jnp.dot(modulated, qkv_w[:, parts[part]], preferred_element_type=F32).T

    def send(first, second, heads, half, sem):
        rows = slice(half * 2 * head_size, (half + 1) * 2 * head_size)
        for i, head in enumerate(heads):
            at = slice(i * head_size, (i + 1) * head_size)
            packed[head, rows, :] = jnp.concatenate([first[at], second[at]], axis=0).astype(BF16)
        block = (slice(heads[0], heads[-1] + 1), rows)
        copy = pltpu.make_async_copy(packed.at[block], out.at[block], sems.at[sem])
        copy.start()
        return copy

    leaving = [send(part_of(0), part_of(1), range(H), 0, 9)]
    values = part_of(2)
    copies[3].wait()
    copies[4].wait()
    gated = (row(gate) * cot[...].astype(F32)).astype(BF16)
    lower = pulled_of(0, gated)
    leaving.append(send(values[:middle], lower, range(H // 2), 1, 10))
    upper = pulled_of(1, gated)
    leaving.append(send(values[middle:], upper, range(H // 2, H), 1, 12))
    for copy in leaving:
        copy.wait()


def project(tokens, shift, scale, gate, qkv_w, out_w, cot):
    tok_rows, width = tokens.shape
    head_size = width // H
    operands = (tokens, shift, scale, gate, cot, out_w, qkv_w)
    hbm = pl.BlockSpec(memory_space=pl.ANY)
    packed = (H, 4 * head_size, tok_rows)
    return pl.pallas_call(
        functools.partial(project_kernel, head_size),
        in_specs=[hbm] * 7,
        out_specs=hbm,
        out_shape=jax.ShapeDtypeStruct(packed, BF16),
        scratch_shapes=[pltpu.VMEM(x.shape, x.dtype) for x in operands]
        + [pltpu.SemaphoreType.DMA((13,)), pltpu.VMEM(packed, BF16)],
        compiler_params=pltpu.CompilerParams(vmem_limit_bytes=PROJECT_LIMIT),
        name="project",
    )(*operands)


def attend_kernel(head_size, group, split, items, weight, *refs):
    if split:
        pairs, held, near, far = refs[:4]
        refs = refs[4:]
    else:
        held, near = refs[:2]
        refs = refs[2:]
    key_rows, value_rows, key_cols, value_cols, key_grad, value_grad, near_flat, sem = refs
    step = pl.program_id(0)
    single = not split and group == items.shape[0]
    load = pltpu.make_async_copy(weight, held, sem)
    chunks = items.shape[0]
    key_chunks = key_rows.shape[0] // LANES
    att_scale = 1.0 / math.sqrt(head_size)
    exponent_scale = att_scale * math.log2(math.e)
    pad = value_rows.shape[1] - head_size

    @pl.when(step == 0)
    def _():
        load.start()
        for s in range(key_chunks):
            if split:
                pair = pairs[s].astype(F32)
            else:
                pair = items[s].astype(F32)[head_size : 3 * head_size]
            at = slice(s * LANES, (s + 1) * LANES)
            keys, values = pair[:head_size], pair[head_size:]
            key_cols[:, at] = keys.astype(BF16)
            value_cols[:, at] = values.astype(BF16)
            key_rows[at, :] = keys.T.astype(BF16)
            value_rows[at, :] = jnp.concatenate(
                [values, jnp.ones((pad, LANES), F32)], axis=0
            ).T.astype(BF16)
        if not single:
            key_grad[...] = jnp.zeros_like(key_grad)
            value_grad[...] = jnp.zeros_like(value_grad)

    block = [items[step * group + g].astype(F32) for g in range(group)]
    queries = jnp.concatenate([b[:head_size] for b in block], axis=1)
    grads = jnp.concatenate([b[3 * head_size :] for b in block], axis=1)
    scores = jnp.dot(key_rows[...], queries.astype(BF16), preferred_element_type=F32)
    row_max = jnp.max(scores, axis=0, keepdims=True)
    exponent = jnp.exp2((scores - row_max) * exponent_scale)
    total = jnp.sum(exponent, axis=0, keepdims=True)
    weights = (exponent * (1.0 / total)).astype(BF16)
    attended = (
        jnp.dot(value_cols[...], weights, preferred_element_type=F32).astype(BF16).astype(F32)
    )
    less = -jnp.sum(attended * grads, axis=0, keepdims=True)
    less_high = less.astype(BF16).astype(F32)
    less_mid = (less - less_high).astype(BF16).astype(F32)
    less_low = less - less_high - less_mid
    place = lax.broadcasted_iota(jnp.int32, (pad, less.shape[1]), 0)
    tail = jnp.where(
        place == 0, less_high, jnp.where(place == 1, less_mid, jnp.where(place == 2, less_low, 0.0))
    )
    centred_grad = jnp.dot(
        value_rows[...],
        jnp.concatenate([grads, tail], axis=0).astype(BF16),
        preferred_element_type=F32,
    )
    score_grad = (weights.astype(F32) * centred_grad * att_scale).astype(BF16)
    query_grad = jnp.dot(key_cols[...], score_grad, preferred_element_type=F32)
    keys_of = jnp.dot(score_grad, queries.T.astype(BF16), preferred_element_type=F32)
    values_of = jnp.dot(weights, grads.T.astype(BF16), preferred_element_type=F32)
    if single:
        for s in range(key_chunks):
            at = slice(s * LANES, (s + 1) * LANES)
            near[s] = jnp.concatenate(
                [attended[:, at], query_grad[:, at], keys_of[at, :].T, values_of[at, :].T], axis=0
            ).astype(BF16)
        load.wait()
        return
    key_grad[...] += keys_of
    value_grad[...] += values_of
    for g in range(group):
        at = slice(g * LANES, (g + 1) * LANES)
        near_flat[step * group + g] = jnp.concatenate(
            [attended[:, at], query_grad[:, at]], axis=0
        )

    @pl.when(step == pl.num_programs(0) - 1)
    def _():
        for s in range(key_chunks):
            at = slice(s * LANES, (s + 1) * LANES)
            grads_of = jnp.concatenate([key_grad[at, :].T, value_grad[at, :].T], axis=0)
            if split:
                far[s] = grads_of
            else:
                near[s] = jnp.concatenate([near_flat[s], grads_of], axis=0).astype(BF16)
        if split:
            near[...] = near_flat[...].astype(BF16)
        load.wait()


def attend(items, weight, pairs=None):
    chunks = items.shape[0]
    head_size = items.shape[1] // 4
    split = pairs is not None
    key_chunks = pairs.shape[0] if split else chunks
    key_len = key_chunks * LANES
    group = math.gcd(chunks, max(1, SCORE_LIMIT // (key_len * LANES)))
    pad = 8
    whole = lambda shape: pl.BlockSpec(shape, lambda i: (0,) * len(shape))
    if split:
        shapes = [
            jax.ShapeDtypeStruct((chunks, 2 * head_size, LANES), BF16),
            jax.ShapeDtypeStruct((key_chunks, 2 * head_size, LANES), F32),
        ]
        operands = (items, weight, pairs)
    else:
        shapes = [jax.ShapeDtypeStruct((chunks, 4 * head_size, LANES), BF16)]
        operands = (items, weight)
    specs = [whole(x.shape) for x in operands]
    specs[1] = pl.BlockSpec(memory_space=pl.ANY)
    shapes = [jax.ShapeDtypeStruct(weight.shape, weight.dtype)] + shapes
    return pl.pallas_call(
        functools.partial(attend_kernel, head_size, group, split),
        grid=(chunks // group,),
        in_specs=specs,
        out_specs=[pl.BlockSpec(memory_space=pltpu.VMEM)] + [whole(x.shape) for x in shapes[1:]],
        out_shape=shapes,
        scratch_shapes=[
            pltpu.VMEM((key_len, head_size), BF16),
            pltpu.VMEM((key_len, head_size + pad), BF16),
            pltpu.VMEM((head_size, key_len), BF16),
            pltpu.VMEM((head_size, key_len), BF16),
            pltpu.VMEM((key_len, head_size), F32),
            pltpu.VMEM((key_len, head_size), F32),
            pltpu.VMEM((chunks, 2 * head_size, LANES), F32),
            pltpu.SemaphoreType.DMA,
        ],
        compiler_params=params(ATTEND_LIMIT),
        name="attend",
    )(*operands)


def gather_kernel(
    head_size, items, tokens, qkv_w, out_w, cot, branch, mod_grad, sums, grad_cols
):
    width = tokens.shape[1]
    flat = [items[head].astype(F32) for head in range(H)]
    back = jnp.zeros((width, tokens.shape[0]), F32)
    for part in range(3):
        at = slice(part * width, (part + 1) * width)
        grad_cols[at, :] = jnp.concatenate(
            [x[(part + 1) * head_size : (part + 2) * head_size] for x in flat], axis=0
        ).astype(BF16)
        back = back + jnp.dot(qkv_w[:, at], grad_cols[at, :], preferred_element_type=F32)
    back = back.T
    att = jnp.concatenate([x[:head_size] for x in flat], axis=0).T.astype(BF16)
    out = jnp.dot(att, out_w[...], preferred_element_type=F32)
    _, normed, _ = normalise(tokens[...])
    branch[...] = out
    mod_grad[...] = back
    sums[...] = jnp.concatenate(
        [
            jnp.sum(back, axis=0, keepdims=True),
            jnp.sum(back * normed, axis=0, keepdims=True),
            jnp.sum(cot[...].astype(F32) * out, axis=0, keepdims=True),
        ],
        axis=0,
    )


def gather(items, tokens, qkv_w, out_w, cot):
    tok_rows, width = tokens.shape
    vmem = pl.BlockSpec(memory_space=pltpu.VMEM)
    return pl.pallas_call(
        functools.partial(gather_kernel, width // H),
        in_specs=[vmem] * 5,
        out_specs=[vmem] * 3,
        out_shape=[
            jax.ShapeDtypeStruct((tok_rows, width), F32),
            jax.ShapeDtypeStruct((tok_rows, width), F32),
            jax.ShapeDtypeStruct((3, width), F32),
        ],
        scratch_shapes=[pltpu.VMEM((3 * width, tok_rows), BF16)],
        compiler_params=pltpu.CompilerParams(vmem_limit_bytes=FINISH_LIMIT),
        name="gather",
    )(items, tokens, qkv_w, out_w, cot)


def finish_kernel(branch, mod_grad, tokens, scale, gate, cot, block_output, grad_input):
    wide, normed, inv_std = normalise(tokens[...])
    block_output[...] = (wide + row(gate) * branch[...]).astype(BF16)
    normed_grad = mod_grad[...] * (1.0 + row(scale))
    first_mean = jnp.mean(normed_grad, axis=1, keepdims=True)
    second_mean = jnp.mean(normed_grad * normed, axis=1, keepdims=True)
    grad_input[...] = (
        cot[...].astype(F32) + inv_std * (normed_grad - first_mean - normed * second_mean)
    ).astype(BF16)


def finish(branch, mod_grad, tokens, scale, gate, cot):
    vmem = pl.BlockSpec(memory_space=pltpu.VMEM)
    return pl.pallas_call(
        finish_kernel,
        in_specs=[vmem] * 6,
        out_specs=[vmem] * 2,
        out_shape=[jax.ShapeDtypeStruct(tokens.shape, BF16)] * 2,
        compiler_params=pltpu.CompilerParams(vmem_limit_bytes=FINISH_LIMIT),
        cost_estimate=pl.CostEstimate(
            flops=30 * tokens.size, transcendentals=0, bytes_accessed=16 * tokens.size
        ),
        name="finish",
    )(branch, mod_grad, tokens, scale, gate, cot)


def from_partner(shard, axis, stride):
    return lax.ppermute(shard, axis, [(i, i ^ stride) for i in range(lax.axis_size(axis))])


def exchange(blocks):
    return lax.all_to_all(blocks, "seq", split_axis=0, concat_axis=0, tiled=True)


def per_device(tokens, shift_cond, scale_cond, gate_cond, qkv_weight, out_weight, cotangent):
    seq_count = lax.axis_size("seq")
    repeat = seq_count // H
    levels = repeat.bit_length() - 1
    tok_rows, width = tokens.shape
    head_size = width // H
    sub_rows = tok_rows // repeat
    packed = project(tokens, shift_cond, scale_cond, gate_cond, qkv_weight, out_weight, cotangent)
    if repeat == 1:
        held, made = attend(exchange(packed), qkv_weight)
        returned = exchange(made)
    else:
        packed = packed.reshape(H, 4 * head_size, repeat, sub_rows).transpose(0, 2, 1, 3)
        landed = exchange(packed.reshape(seq_count, 4 * head_size, sub_rows))
        items = landed.reshape(H, repeat, 4 * head_size, sub_rows).transpose(0, 2, 1, 3)
        items = items.reshape(H, 4 * head_size, tok_rows)
        pairs = items[:, head_size : 3 * head_size]
        for level in range(levels):
            pairs = jnp.concatenate([pairs, from_partner(pairs, "seq", 1 << level)], axis=0)
        held, near, far = attend(items, qkv_weight, pairs)
        for level in reversed(range(levels)):
            middle = far.shape[0] // 2
            far = far[:middle] + from_partner(far[middle:], "seq", 1 << level)
        made = jnp.concatenate([near, far.astype(BF16)], axis=1)
        made = made.reshape(H, 4 * head_size, repeat, sub_rows).transpose(0, 2, 1, 3)
        back = exchange(made.reshape(seq_count, 4 * head_size, sub_rows))
        returned = back.reshape(H, repeat, 4 * head_size, sub_rows).transpose(0, 2, 1, 3)
        returned = returned.reshape(H, 4 * head_size, tok_rows)
    branch, mod_grad, sums = gather(returned, tokens, held, out_weight, cotangent)
    block_output, grad_input = finish(
        branch, mod_grad, tokens, scale_cond, gate_cond, cotangent
    )
    stride = 1
    while stride < seq_count:
        if 4 * stride <= seq_count:
            first, second, third = (from_partner(sums, "seq", k * stride) for k in (1, 2, 3))
            sums = (sums + first) + (second + third)
            stride *= 4
        else:
            sums = sums + from_partner(sums, "seq", stride)
            stride *= 2
    return (block_output, grad_input, sums / math.sqrt(tok_rows * seq_count))


def solution(mesh):
    return jax.shard_map(
        per_device,
        mesh=mesh,
        in_specs=(
            P(("groups", "seq"), None),
            P("groups"),
            P("groups"),
            P("groups"),
            P(),
            P(),
            P(("groups", "seq"), None),
        ),
        out_specs=(P(("groups", "seq"), None), P(("groups", "seq"), None), P("groups", None)),
        check_vma=False,
    )
```
